768 devices in a mesh: pipe: 8 (over y_hi, core), dp: 24 (over y_lo, z), tensor: 4 (over x).
Axes of the slice: x: 4, y: 8 (y_hi: 4, y_lo: 2; y = y_hi * 2 + y_lo), z: 12, core: 2. Of those that a mesh axis runs over, the one named last changes fastest.
Arguments:
- pooled: bfloat16 [192, 256, 5120], P(('pipe', 'dp')), may hold values from -10 to 10
- layer_norm_gain: float32 [5120], replicated, may hold values from 0.1 to 1.9
- w_first: bfloat16 [5120, 2048], P(None, 'tensor'), may hold values from -0.078125 to 0.078125
- w_second: bfloat16 [2048, 1024], P('tensor'), may hold values from -0.125 to 0.125
- teacher: bfloat16 [192, 1024], P(('pipe', 'dp')), may hold values from -6 to 6
Outputs:
- loss: float32 [], replicated
- pooled_grad: bfloat16 [192, 256, 5120], P(('pipe', 'dp'), None, 'tensor')
The draws below stay inside these ranges and needn't reach their ends.
All inputs are finite; a program needn't handle non-finite values.
Results may differ from the reference program's by a relative error of at most 0.012.
Values may be sent and summed in bfloat16 or wider, within the bound.
A program may use at most 64 MiB of HBM per device.

```python
import jax
import jax.numpy as jnp
from jax import lax

D = 5120
HID = 2048
EMB = 1024
PATCHES = 256
BATCH = 192


def draw_pooled(key, part):
    shared_key = jax.random.fold_in(key, 11)
    token_key = jax.random.fold_in(key, 12)
    shared = 1.5 * jax.random.truncated_normal(shared_key, -4.0, 4.0, (BATCH, 1, D), jnp.float32)
    tokens = jax.random.truncated_normal(token_key, -4.0, 4.0, (BATCH, PATCHES, D), jnp.float32)
    return (shared + tokens).astype(jnp.bfloat16)


def shard_levels(stream_key, shape, split, least, top_value):
    def one(axis_at, blocks):
        heights = jax.random.uniform(jax.random.fold_in(jax.random.fold_in(stream_key, 6), axis_at), (blocks,), jnp.float32, least / len(split), top_value / len(split))
        return jnp.repeat(jnp.exp(heights), shape[axis_at] // blocks).reshape((-1,) + (1,) * (len(shape) - axis_at - 1))

    loudness = one(*split[0])
    for cut in split[1:]:
        loudness = loudness * one(*cut)
    return loudness


def bell_draw(own_key, extent, width, most, pieces=(), kind=jnp.bfloat16):
    result = width * jax.random.normal(own_key, extent, jnp.float32)
    if pieces:
        result = result * shard_levels(own_key, extent, pieces, -0.22, 0.18)
    return jnp.clip(result, -most, most).astype(kind)


def setup_inputs(seed: int = 0) -> dict:
    streams_of = jax.random.split(jax.random.key(seed), 6)
    pooled = draw_pooled(jax.random.fold_in(streams_of[5], 71), 0)
    layer_norm_gain = jnp.clip(1.0 + 0.18 * jax.random.normal(streams_of[1], (D,), jnp.float32), 0.1, 1.9)
    w_first = bell_draw(streams_of[2], (D, HID), D ** -0.5, 0.078125, ((1, 4),))
    w_second = bell_draw(streams_of[3], (HID, EMB), HID ** -0.5, 0.125, ((0, 4),))
    teacher = bell_draw(streams_of[4], (BATCH, EMB), 1.0, 6.0, ((0, 192),))
    return {"pooled": pooled, "layer_norm_gain": layer_norm_gain, "w_first": w_first, "w_second": w_second, "teacher": teacher}


student_scale = 10.0
teacher_scale = 20.0
masked_value = -1000000000.0

def gelu_slope(pre):
    return 0.5 * (1.0 + lax.erf(pre * 0.7071067811865476)) + pre * jnp.exp(-0.5 * pre * pre) * 0.3989422804014327

def row_lse(logits):
    top = lax.optimization_barrier(jnp.max(logits, axis=-1, keepdims=True))
    return top + jnp.log(lax.optimization_barrier(jnp.sum(jnp.exp(logits - top), axis=-1, keepdims=True)))

def layer_norm_pieces(picture_input, layer_norm_gain):
    values = picture_input.astype(jnp.float32)
    centered_values = values - lax.optimization_barrier(jnp.mean(values, axis=-1, keepdims=True))
    inverse_deviation = lax.rsqrt(lax.optimization_barrier(jnp.mean(centered_values * centered_values, axis=-1, keepdims=True)) + 1e-05)
    standardized_input = centered_values * inverse_deviation
    normalized_rows = (standardized_input * layer_norm_gain).astype(jnp.bfloat16)
    return (standardized_input, inverse_deviation, normalized_rows)

def reference(pooled, layer_norm_gain, w_first, w_second, teacher):

    def forward_one(picture_input):
        standardized_input, inverse_deviation, normalized_rows = layer_norm_pieces(picture_input, layer_norm_gain)
        pre = jnp.dot(normalized_rows, w_first, preferred_element_type=jnp.float32)
        act = jax.nn.gelu(pre, approximate=False)
        return lax.optimization_barrier(jnp.mean(act, axis=0)).astype(jnp.bfloat16)
    pools = lax.map(forward_one, pooled)
    student = jnp.dot(pools, w_second, preferred_element_type=jnp.float32)
    norm_s = jnp.sqrt(lax.optimization_barrier(jnp.sum(student * student, axis=-1, keepdims=True)) + 1e-06)
    unit32 = student / norm_s
    unit = unit32.astype(jnp.bfloat16)
    tvals = teacher.astype(jnp.float32)
    tunit = (tvals / jnp.sqrt(lax.optimization_barrier(jnp.sum(tvals * tvals, axis=-1, keepdims=True)) + 1e-06)).astype(jnp.bfloat16)
    count = pooled.shape[0]
    index = jnp.arange(count, dtype=jnp.int32)
    self_mask = index[:, None] == index[None, :]
    s_log = jnp.where(self_mask, masked_value, student_scale * jnp.dot(unit, unit.T, preferred_element_type=jnp.float32))
    t_log = jnp.where(self_mask, masked_value, teacher_scale * jnp.dot(tunit, tunit.T, preferred_element_type=jnp.float32))
    log_q = s_log - row_lse(s_log)
    log_p = t_log - row_lse(t_log)
    prob_p = jnp.exp(log_p)
    prob_q = jnp.exp(log_q)
    terms = jnp.where(self_mask, 0.0, prob_p * (log_p - log_q))
    loss = jnp.sum(terms) / count
    d_log = ((prob_q - prob_p) / count).astype(jnp.bfloat16)
    d_unit = student_scale * (jnp.dot(d_log, unit, preferred_element_type=jnp.float32) + jnp.dot(d_log.T, unit, preferred_element_type=jnp.float32))
    along = lax.optimization_barrier(jnp.sum(unit32 * d_unit, axis=-1, keepdims=True))
    d_student = ((d_unit - unit32 * along) / norm_s).astype(jnp.bfloat16)
    d_pools = jnp.dot(d_student, w_second.T, preferred_element_type=jnp.float32)
    patches = pooled.shape[1]

    def backward_one(pair):
        picture_input, d_pool = pair
        standardized_input, inverse_deviation, normalized_rows = layer_norm_pieces(picture_input, layer_norm_gain)
        pre = jnp.dot(normalized_rows, w_first, preferred_element_type=jnp.float32)
        d_pre = ((d_pool / patches)[None, :] * gelu_slope(pre)).astype(jnp.bfloat16)
        d_normed = jnp.dot(d_pre, w_first.T, preferred_element_type=jnp.float32)
        gradient_list = d_normed * layer_norm_gain
        final_output = inverse_deviation * (gradient_list - lax.optimization_barrier(jnp.mean(gradient_list, axis=-1, keepdims=True)) - standardized_input * lax.optimization_barrier(jnp.mean(gradient_list * standardized_input, axis=-1, keepdims=True)))
        return final_output.astype(jnp.bfloat16)
    pooled_grad = lax.map(backward_one, (pooled, d_pools))
    return (loss, pooled_grad)
```

```python
import functools

import jax
import jax.numpy as jnp
from jax import lax
from jax.experimental import pallas as pl
from jax.experimental.pallas import tpu as pltpu
from jax.sharding import Mesh
from jax.sharding import PartitionSpec as P

IMAGES = ("yh", "core", "yl", "z")
MESH = pl.DeviceIdType.MESH

student_scale = 10.0
teacher_scale = 20.0
masked_value = -1000000000.0
F32, BF16 = jnp.float32, jnp.bfloat16


def gelu_slope(pre):
    return (
        0.5 * (1.0 + lax.erf(pre * 0.7071067811865476))
        + pre * jnp.exp(-0.5 * pre * pre) * 0.3989422804014327
    )


def as_tile(row):
    return jnp.concatenate([row[:, k * 128 : (k + 1) * 128] for k in range(8)], axis=0)


class Place:
    def __init__(self, sizes):
        self.sizes = sizes
        self.x, self.z, self.c = (lax.axis_index(a) for a in ("x", "z", "core"))
        self.nx, self.nz, self.nc = sizes["x"], sizes["z"], sizes["core"]
        self.nl = sizes["yl"]
        self.ny = sizes["yh"] * sizes["yl"]
        self.y = lax.axis_index("yh") * self.nl + lax.axis_index("yl")
        self.row = (self.c * self.ny + self.y) * self.nz + self.z

    def at_x(self, d):
        return lax.rem(self.x + d, self.nx)

    def at_y(self, d):
        return lax.rem(self.y + d, self.ny)

    def at_z(self, d):
        return lax.rem(self.z + d, self.nz)

    def to_y(self, yy):
        return {"yh": yy // self.nl, "yl": lax.rem(yy, self.nl)}


def remote(src, dst, ss, rs, where):
    return pltpu.make_async_remote_copy(
        src_ref=src, dst_ref=dst, send_sem=ss, recv_sem=rs, device_id=where, device_id_type=MESH
    )


def relation_kernel(sizes, part, tea, dst_out, loss_out, xbuf, ub, tb, wide, U, T,
                    xs, xr, uzs, uzr, uys, uyr, ucs, ucr, tzs, tzr, tys, tyr, tcs, tcr):
    me = Place(sizes)
    x, y, z, c = me.x, me.y, me.z, me.c
    nx, ny, nz = me.nx, me.ny, me.nz
    count = 2 * ny * nz

    barrier = pltpu.get_barrier_semaphore()
    peers = (
        [{"x": me.at_x(d)} for d in range(1, nx)]
        + [{"z": me.at_z(d)} for d in range(1, nz)]
        + [me.to_y(me.at_y(d)) for d in range(1, ny)]
        + [{"core": 1 - c}]
    )
    for p in peers:
        pl.semaphore_signal(barrier, inc=1, device_id=p, device_id_type=MESH)

    tvals = tea[...].astype(F32)
    tunit = tvals / jnp.sqrt(jnp.sum(tvals * tvals, axis=-1, keepdims=True) + 1e-06)
    tb[c, y, z] = as_tile(tunit).astype(BF16)
    xbuf[x] = part[...]
    pl.semaphore_wait(barrier, len(peers))

    waits = []

    def send(*a):
        cp = remote(*a)
        cp.start()
        waits.append(cp)

    for d in range(1, nx):
        send(xbuf.at[x], xbuf.at[x], xs.at[d], xr.at[x], {"x": me.at_x(d)})

    def z_send(buf, ss, rs):
        for d in range(1, nz):
            send(buf.at[c, y, z], buf.at[c, y, z], ss.at[d], rs.at[z], {"z": me.at_z(d)})

    def z_wait(buf, ss, rs):
        for d in range(1, nz):
            zz = me.at_z(d)
            remote(buf.at[c, y, zz], buf.at[c, y, zz], ss.at[0], rs.at[zz], {"z": zz}).wait_recv()

    def y_send(buf, ss, rs):
        for d in (4, 3, 5, 2, 6, 1, 7):
            send(buf.at[c, y], buf.at[c, y], ss.at[d], rs.at[y], me.to_y(me.at_y(d)))

    def c_send(buf, ss, rs, yy, d):
        send(buf.at[c, yy], buf.at[c, yy], ss.at[d], rs.at[yy], {"core": 1 - c})

    def y_wait_and_pass(buf, ss, rs, cs, cr):
        c_send(buf, cs, cr, y, 0)
        for d in (1, 7, 2, 6, 3, 5, 4):
            yy = me.at_y(d)
            remote(buf.at[c, yy], buf.at[c, yy], ss.at[0], rs.at[yy], me.to_y(yy)).wait_recv()
            c_send(buf, cs, cr, yy, d)

    def c_wait(buf, cs, cr):
        for yy in range(ny):
            remote(buf.at[1 - c, yy], buf.at[1 - c, yy], cs.at[0], cr.at[yy], {"core": 1 - c}).wait_recv()

    def assemble(buf, out):
        wide[...] = buf[...].astype(F32).reshape(count * 8, 128)
        for s in range(8):
            out[:, s * 128 : (s + 1) * 128] = wide[pl.ds(s, count, stride=8), :].astype(BF16)

    z_send(tb, tzs, tzr)
    for d in range(1, nx):
        xx = me.at_x(d)
        remote(xbuf.at[xx], xbuf.at[xx], xs.at[0], xr.at[xx], {"x": xx}).wait_recv()
    student = xbuf[0]
    for k in range(1, nx):
        student = student + xbuf[k]
    norm_s = jnp.sqrt(jnp.sum(student * student, axis=-1, keepdims=True) + 1e-06)
    unit32 = student / norm_s
    ub[c, y, z] = as_tile(unit32).astype(BF16)
    z_send(ub, uzs, uzr)
    z_wait(tb, tzs, tzr)
    z_wait(ub, uzs, uzr)
    y_send(ub, uys, uyr)
    y_send(tb, tys, tyr)
    y_wait_and_pass(ub, uys, uyr, ucs, ucr)
    y_wait_and_pass(tb, tys, tyr, tcs, tcr)
    c_wait(tb, tcs, tcr)
    assemble(tb, T)
    c_wait(ub, ucs, ucr)
    assemble(ub, U)

    down = lax.broadcasted_iota(jnp.int32, (count, count), 0)
    across = lax.broadcasted_iota(jnp.int32, (count, count), 1)
    diagonal = down == across
    lane = lax.broadcasted_iota(jnp.int32, (1, count), 1)

    def similarity(mat, scale):
        a = mat[...]
        s = lax.dot_general(a, a, (((1,), (1,)), ((), ())), preferred_element_type=F32)
        s = jnp.where(diagonal, masked_value, scale * s)
        top = jnp.max(s, axis=1, keepdims=True)
        lse = top + jnp.log(jnp.sum(jnp.exp(s - top), axis=1, keepdims=True))
        topr = jnp.max(s, axis=0, keepdims=True)
        lse_r = topr + jnp.log(jnp.sum(jnp.exp(s - topr), axis=0, keepdims=True))
        own = jnp.sum(jnp.where(down == me.row, s, 0.0), axis=0, keepdims=True)
        lse_own = jnp.sum(jnp.where(lane == me.row, lse_r, 0.0), axis=1, keepdims=True)
        return s - lse, jnp.exp(own - lse_own), jnp.exp(own - lse_r)

    log_p, p_row, p_col = similarity(T, teacher_scale)
    log_q, q_row, q_col = similarity(U, student_scale)
    prob_p = jnp.exp(log_p)
    terms = jnp.where(diagonal, 0.0, prob_p * (log_p - log_q))
    loss_out[...] = jnp.sum(jnp.sum(terms, axis=1, keepdims=True), axis=0, keepdims=True) / count
    sub = lax.broadcasted_iota(jnp.int32, (16, count), 0)
    d_row = (q_row - p_row) / count
    d_col = (q_col - p_col) / count
    both = jnp.where(sub == 0, d_row, jnp.where(sub == 1, d_col, 0.0)).astype(BF16)
    rows = jnp.dot(both, U[...], preferred_element_type=F32)
    d_unit = student_scale * jnp.sum(rows, axis=0, keepdims=True)
    along = jnp.sum(unit32 * d_unit, axis=-1, keepdims=True)
    dst_out[...] = (d_unit - unit32 * along) / norm_s
    for cp in waits:
        cp.wait_send()


def relation(sizes, part, tea):
    ny, nz, nx = sizes["yh"] * sizes["yl"], sizes["z"], sizes["x"]
    count, width = 2 * ny * nz, part.shape[-1]
    dma = lambda n: pltpu.SemaphoreType.DMA((n,))
    return pl.pallas_call(
        functools.partial(relation_kernel, sizes),
        out_shape=(jax.ShapeDtypeStruct((1, width), F32), jax.ShapeDtypeStruct((1, 1), F32)),
        in_specs=[pl.BlockSpec(memory_space=pltpu.VMEM)] * 2,
        out_specs=(pl.BlockSpec(memory_space=pltpu.VMEM),) * 2,
        scratch_shapes=[
            pltpu.VMEM((nx, 1, width), F32),
            pltpu.VMEM((2, ny, nz, 8, 128), BF16),
            pltpu.VMEM((2, ny, nz, 8, 128), BF16),
            pltpu.VMEM((count * 8, 128), F32),
            pltpu.VMEM((count, width), BF16),
            pltpu.VMEM((count, width), BF16),
            dma(nx), dma(nx),
            dma(nz), dma(nz), dma(ny), dma(ny), dma(ny), dma(ny),
            dma(nz), dma(nz), dma(ny), dma(ny), dma(ny), dma(ny),
        ],
        compiler_params=pltpu.CompilerParams(collective_id=0, has_side_effects=True),
    )(part, tea)


def on_device(sizes, pooled, layer_norm_gain, w_first, w_second, teacher):
    images, patches, width = pooled.shape
    values = pooled.reshape(images * patches, width).astype(F32)
    centered_values = values - jnp.mean(values, axis=-1, keepdims=True)
    inverse_deviation = lax.rsqrt(
        jnp.mean(centered_values * centered_values, axis=-1, keepdims=True) + 1e-05
    )
    standardized_input = centered_values * inverse_deviation
    normalized_rows = (standardized_input * layer_norm_gain).astype(BF16)
    pre = jnp.dot(normalized_rows, w_first, preferred_element_type=F32)
    act = jax.nn.gelu(pre, approximate=False)
    pools = jnp.mean(act.reshape(images, patches, -1), axis=1).astype(BF16)
    partial_emb = jnp.dot(pools, w_second, preferred_element_type=F32)
    d_student, loss = relation(sizes, partial_emb, teacher)
    d_student = d_student.astype(BF16)
    d_pool = jnp.dot(d_student, w_second.T, preferred_element_type=F32)
    d_pre32 = (d_pool / patches) * gelu_slope(pre)
    d_pre = d_pre32.astype(BF16)
    partial_grad = lax.dot_general(
        d_pre, w_first, (((1,), (1,)), ((), ())), preferred_element_type=F32
    ).astype(BF16)
    n = sizes["x"]
    tiles = jnp.moveaxis(partial_grad.reshape(patches, n, width // n), 1, 0)
    arrived = lax.all_to_all(tiles, "x", split_axis=0, concat_axis=0, tiled=True)
    d_cols = jnp.sum(arrived.astype(F32), axis=0)
    v = jnp.dot(layer_norm_gain[None, :], w_first.astype(F32), precision=lax.Precision.HIGHEST)
    d_pre_f = d_pre.astype(F32)
    both = jnp.stack([jnp.sum(d_pre_f * v, axis=-1), jnp.sum(d_pre_f * pre, axis=-1)])
    both = lax.all_to_all(jnp.broadcast_to(both[None], (n, *both.shape)), "x", 0, 0, tiled=True).sum(0)
    portion = width // n
    offset = lax.axis_index("x") * portion
    gain_cols = lax.dynamic_slice_in_dim(layer_norm_gain, offset, portion, 0)
    standardized_columns = lax.dynamic_slice_in_dim(standardized_input, offset, portion, 1)
    final_output = inverse_deviation * (
        d_cols * gain_cols - (both[0] / width)[:, None] - standardized_columns * (both[1] / width)[:, None]
    )
    return (loss[0, 0], final_output.reshape(images, patches, portion).astype(BF16))


def solution(mesh):
    names = ("yh", "core", "yl", "z", "x")
    split = Mesh(mesh.devices.reshape(4, 2, 2, 12, mesh.shape["tensor"]), names)
    in_specs = (P(IMAGES, None, None), P(), P(None, "x"), P("x", None), P(IMAGES, None))
    out_specs = (P(), P(IMAGES, None, "x"))
    return jax.shard_map(
        functools.partial(on_device, dict(split.shape)),
        mesh=split, in_specs=in_specs, out_specs=out_specs, check_vma=False,
    )
```

```python
import functools

import jax
import jax.numpy as jnp
from jax import lax
from jax.experimental import pallas as pl
from jax.experimental.pallas import tpu as pltpu
from jax.sharding import Mesh
from jax.sharding import PartitionSpec as P

IMAGES = ("yh", "core", "yl", "z")
MESH = pl.DeviceIdType.MESH

student_scale = 10.0
teacher_scale = 20.0
masked_value = -1000000000.0
F32, BF16 = jnp.float32, jnp.bfloat16
NT = (((1,), (1,)), ((), ()))
LANES = 128
BLOCK = 64


def as_tile(row):
    return jnp.concatenate([row[:, k * 128 : (k + 1) * 128] for k in range(8)], axis=0)


def normal_cdf(v):
    return 0.5 * (1.0 + lax.erf(v * 0.7071067811865476))


class Place:
    def __init__(self, sizes):
        self.x, self.z, self.c = (lax.axis_index(a) for a in ("x", "z", "core"))
        self.nx, self.nz = sizes["x"], sizes["z"]
        self.nl = sizes["yl"]
        self.ny = sizes["yh"] * sizes["yl"]
        self.y = lax.axis_index("yh") * self.nl + lax.axis_index("yl")
        self.row = (self.c * self.ny + self.y) * self.nz + self.z

    def at_x(self, d):
        return lax.rem(self.x + d, self.nx)

    def at_y(self, d):
        return lax.rem(self.y + d, self.ny)

    def at_z(self, d):
        return lax.rem(self.z + d, self.nz)

    def to_y(self, yy):
        return {"yh": yy // self.nl, "yl": lax.rem(yy, self.nl)}


def remote(src, dst, ss, rs, where):
    return pltpu.make_async_remote_copy(
        src_ref=src, dst_ref=dst, send_sem=ss, recv_sem=rs, device_id=where, device_id_type=MESH
    )


def step_kernel(sizes, pooled, gain, w1, w2, tea, out, loss_out,
                xv, nv, wv, w2v, wc, pv, sb, sl, xh, acc, meanv, rstdv,
                xbuf, cbuf, ub, tb, wide, U, T,
                local, xs, xr, cs, cr, ps, pr,
                uzs, uzr, uys, uyr, ucs, ucr, tzs, tzr, tys, tyr, tcs, tcr,
                wxs, wxr, wzs, wzr, wys, wyr, wds, wdr):
    me = Place(sizes)
    x, y, z, c = me.x, me.y, me.z, me.c
    nx, ny, nz = me.nx, me.ny, me.nz
    count = 2 * ny * nz
    tokens, width = xv.shape
    hid = wv.shape[1]
    emb = w2v.shape[1]
    cols = width // nx
    tiles = width // LANES

    barrier = pltpu.get_barrier_semaphore()
    peers = (
        [{"x": me.at_x(d)} for d in range(1, nx)]
        + [{"z": me.at_z(d)} for d in range(1, nz)]
        + [me.to_y(me.at_y(d)) for d in range(1, ny)]
        + [{"core": 1 - c}]
    )
    for p in peers:
        pl.semaphore_signal(barrier, inc=1, device_id=p, device_id_type=MESH)

    get_x = pltpu.make_async_copy(pooled.at[0], xv, local.at[0])
    get_x.start()
    get_w = []
    for k in range(nx):
        rows = pl.ds(k * cols, cols)
        get_w.append(pltpu.make_async_copy(w1.at[rows], wv.at[rows], local.at[1 + k]))
        get_w[-1].start()
    get_w2 = pltpu.make_async_copy(w2, w2v, local.at[1 + nx])
    get_w2.start()

    waits = []

    def send(*a):
        cp = remote(*a)
        cp.start()
        waits.append(cp)

    def arrive(ref, ss, rs, where):
        remote(ref, ref, ss, rs, where).wait_recv()

    tvals = tea[...].astype(F32)
    tunit = tvals / jnp.sqrt(jnp.sum(tvals * tvals, axis=-1, keepdims=True) + 1e-06)
    tb[c, y, z] = as_tile(tunit).astype(BF16)
    g = gain[...]
    g_hi = g.astype(BF16)
    g_lo = (g - g_hi.astype(F32)).astype(BF16)
    sub16 = lax.broadcasted_iota(jnp.int32, (16, width), 0)
    nv[tokens:, :] = jnp.where(
        sub16 == 0, g_hi.astype(F32), jnp.where(sub16 == 1, g_lo.astype(F32), 0.0)
    ).astype(BF16)

    get_x.wait()
    ones = jnp.ones((cols, LANES), BF16)
    total = jnp.dot(xv[:, :cols], ones, preferred_element_type=F32)
    for k in range(1, nx):
        total += jnp.dot(xv[:, k * cols : (k + 1) * cols], ones, preferred_element_type=F32)
    meanv[...] = total / width

    @pl.loop(0, tokens // BLOCK)
    def _(i):
        r = pl.ds(pl.multiple_of(i * BLOCK, BLOCK), BLOCK)
        m = meanv[r, :]
        squares = jnp.zeros((BLOCK, LANES), F32)
        for k in range(tiles):
            dev = xv[r, k * LANES : (k + 1) * LANES].astype(F32) - m
            squares += dev * dev
        var = jnp.sum(squares, axis=1, keepdims=True) / width
        rstdv[r, :] = jnp.broadcast_to(lax.rsqrt(var + 1e-05), (BLOCK, LANES))

    pl.semaphore_wait(barrier, len(peers))

    def z_send(buf, ss, rs):
        for d in range(1, nz):
            send(buf.at[c, y, z], buf.at[c, y, z], ss.at[d], rs.at[z], {"z": me.at_z(d)})

    def z_wait(buf, ss, rs):
        for d in range(1, nz):
            zz = me.at_z(d)
            arrive(buf.at[c, y, zz], ss.at[0], rs.at[zz], {"z": zz})

    def y_send(buf, ss, rs):
        for d in (4, 3, 5, 2, 6, 1, 7):
            send(buf.at[c, y], buf.at[c, y], ss.at[d], rs.at[y], me.to_y(me.at_y(d)))

    def c_send(buf, ss, rs, yy, d):
        send(buf.at[c, yy], buf.at[c, yy], ss.at[d], rs.at[yy], {"core": 1 - c})

    def y_wait_and_pass(buf, ss, rs, css, crs):
        c_send(buf, css, crs, y, 0)
        for d in (1, 7, 2, 6, 3, 5, 4):
            yy = me.at_y(d)
            arrive(buf.at[c, yy], ss.at[0], rs.at[yy], me.to_y(yy))
            c_send(buf, css, crs, yy, d)

    def c_wait(buf, css, crs):
        for yy in range(ny):
            arrive(buf.at[1 - c, yy], css.at[0], crs.at[yy], {"core": 1 - c})

    quarter = cols // 4
    piece = quarter // 2
    half = piece // 2
    color = lax.rem(2 * y + z, 4)

    def place(k, part=0, length=piece):
        q = lax.rem(color + k, 4)
        return pl.ds(pl.multiple_of(q * quarter + c * piece + part, 16), length)

    for d in range(1, nx):
        xx = me.at_x(d)
        start = pl.multiple_of(xx * cols + color * quarter + c * piece, 16)
        send(w1.at[pl.ds(start, piece)], wc.at[x, place(0)], wxs.at[d], wxr.at[x], {"x": xx})
    z_send(tb, tzs, tzr)

    @pl.loop(0, tokens // BLOCK)
    def _(i):
        r = pl.ds(pl.multiple_of(i * BLOCK, BLOCK), BLOCK)
        m, s = meanv[r, :], rstdv[r, :]
        for k in range(tiles):
            t = slice(k * LANES, (k + 1) * LANES)
            nv[r, t] = ((xv[r, t].astype(F32) - m) * s * gain[:, t]).astype(BF16)

    for k in range(nx):
        get_w[k].wait()
        t = slice(k * cols, (k + 1) * cols)
        part = jnp.dot(nv[:, t], wv[t, :], preferred_element_type=F32)
        if k == 0:
            pv[...] = part
        else:
            pv[...] += part

    pool = []
    for k in range(hid // LANES):
        t = slice(k * LANES, (k + 1) * LANES)

        def body(i, total, t=t):
            r = pl.ds(pl.multiple_of(i * BLOCK, BLOCK), BLOCK)
            p = pv[r, t]
            sb[x, r, t] = p.astype(BF16)
            act = p * normal_cdf(p)
            for j in range(BLOCK // 8):
                total += act[j * 8 : (j + 1) * 8]
            return total

        total = lax.fori_loop(0, tokens // BLOCK, body, jnp.zeros((8, LANES), F32))
        pool.append(jnp.sum(total, axis=0, keepdims=True))
    pool = jnp.concatenate(pool, axis=1) / tokens
    get_w2.wait()
    pool16 = jnp.broadcast_to(pool, (16, hid)).astype(BF16)
    xbuf[x, :, :emb] = jnp.dot(pool16, w2v[...], preferred_element_type=F32)[:1]
    xbuf[x, :, emb:] = pv[tokens : tokens + 1, :] + pv[tokens + 1 : tokens + 2, :]

    for d in range(1, nx):
        send(xbuf.at[x], xbuf.at[x], xs.at[d], xr.at[x], {"x": me.at_x(d)})
    for d in (2, 1, 3):
        send(sb.at[x], sb.at[x], ps.at[d], pr.at[x], {"x": me.at_x(d)})
    z_wait(tb, tzs, tzr)
    y_send(tb, tys, tyr)
    for d in range(1, nx):
        xx = me.at_x(d)
        arrive(xbuf.at[xx], xs.at[0], xr.at[xx], {"x": xx})
    student = xbuf[0, :, :emb]
    for k in range(1, nx):
        student = student + xbuf[k, :, :emb]
    norm_s = jnp.sqrt(jnp.sum(student * student, axis=-1, keepdims=True) + 1e-06)
    unit32 = student / norm_s
    ub[c, y, z] = as_tile(unit32).astype(BF16)
    z_send(ub, uzs, uzr)

    for d in range(1, nx):
        xx = me.at_x(d)
        block = wc.at[xx, place(0)]
        arrive(block, wxs.at[0], wxr.at[xx], {"x": xx})
        send(block, block, wzs.at[0, d], wzr.at[0, d], {"z": me.at_z(1)})
        send(block, block, wzs.at[1, d], wzr.at[1, d], {"z": me.at_z(nz - 1)})
        low, high = wc.at[xx, place(0, 0, half)], wc.at[xx, place(0, half, half)]
        send(low, low, wys.at[0, d], wyr.at[0, d], me.to_y(me.at_y(1)))
        send(high, high, wys.at[1, d], wyr.at[1, d], me.to_y(me.at_y(ny - 1)))
        send(block, block, wds.at[0, d], wdr.at[0, d], {"core": 1 - c})

    def own_columns(k):
        return pl.ds(pl.multiple_of(x * cols + k * LANES, LANES), LANES)

    for k in range(cols // LANES):
        t = slice(k * LANES, (k + 1) * LANES)
        xh[:, t] = (xv[:, own_columns(k)].astype(F32) - meanv[...]) * rstdv[...]

    def slope_of(xx):
        for k in range(hid // LANES):
            t = slice(k * LANES, (k + 1) * LANES)

            @pl.loop(0, tokens // BLOCK)
            def _(i, t=t):
                r = pl.ds(pl.multiple_of(i * BLOCK, BLOCK), BLOCK)
                p = sb[xx, r, t].astype(F32)
                s = normal_cdf(p) + p * jnp.exp(-0.5 * p * p) * 0.3989422804014327
                sl[xx, r, t] = s.astype(BF16)

    slope_of(x)
    y_wait_and_pass(tb, tys, tyr, tcs, tcr)
    z_wait(ub, uzs, uzr)
    y_send(ub, uys, uyr)

    def assemble(buf, dst):
        wide[...] = buf[...].astype(F32).reshape(count * 8, LANES)
        for s in range(8):
            dst[:, s * LANES : (s + 1) * LANES] = wide[pl.ds(s, count, stride=8), :].astype(BF16)

    down = lax.broadcasted_iota(jnp.int32, (count, count), 0)
    across = lax.broadcasted_iota(jnp.int32, (count, count), 1)
    diagonal = down == across
    lane = lax.broadcasted_iota(jnp.int32, (1, count), 1)

    def similarity(mat, scale):
        a = mat[...]
        s = lax.dot_general(a, a, NT, preferred_element_type=F32)
        s = jnp.where(diagonal, masked_value, scale * s)
        topr = jnp.max(s, axis=0, keepdims=True)
        lse_r = topr + jnp.log(jnp.sum(jnp.exp(s - topr), axis=0, keepdims=True))
        own = jnp.sum(jnp.where(down == me.row, s, 0.0), axis=0, keepdims=True)
        lse_own = jnp.sum(jnp.where(lane == me.row, lse_r, 0.0), axis=1, keepdims=True)
        return s, jnp.exp(own - lse_own), jnp.exp(own - lse_r)

    def log_probabilities(s):
        top = jnp.max(s, axis=1, keepdims=True)
        return s - (top + jnp.log(jnp.sum(jnp.exp(s - top), axis=1, keepdims=True)))

    c_wait(tb, tcs, tcr)
    assemble(tb, T)
    t_log, p_row, p_col = similarity(T, teacher_scale)
    log_p = log_probabilities(t_log)
    prob_p = jnp.exp(log_p)

    def pre_arrives(d):
        xx = me.at_x(d)
        arrive(sb.at[xx], ps.at[0], pr.at[xx], {"x": xx})
        slope_of(xx)

    pre_arrives(1)
    y_wait_and_pass(ub, uys, uyr, ucs, ucr)

    for d in range(1, nx):
        xx = me.at_x(d)
        before, after = wc.at[xx, place(3)], wc.at[xx, place(1)]
        arrive(before, wzs.at[0, 0], wzr.at[0, d], {"z": me.at_z(nz - 1)})
        send(before, before, wds.at[1, d], wdr.at[1, d], {"core": 1 - c})
        arrive(after, wzs.at[0, 0], wzr.at[1, d], {"z": me.at_z(1)})
        send(after, after, wds.at[2, d], wdr.at[2, d], {"core": 1 - c})
        arrive(wc.at[xx, place(2, 0, half)], wys.at[0, 0], wyr.at[0, d], me.to_y(me.at_y(ny - 1)))
        arrive(wc.at[xx, place(2, half, half)], wys.at[0, 0], wyr.at[1, d], me.to_y(me.at_y(1)))
        other = wc.at[xx, place(2)]
        send(other, other, wds.at[3, d], wdr.at[3, d], {"core": 1 - c})

    c_wait(ub, ucs, ucr)
    assemble(ub, U)
    s_log, q_row, q_col = similarity(U, student_scale)
    sub = lax.broadcasted_iota(jnp.int32, (16, count), 0)
    d_row = (q_row - p_row) / count
    d_col = (q_col - p_col) / count
    both = jnp.where(sub == 0, d_row, jnp.where(sub == 1, d_col, 0.0)).astype(BF16)
    rows = jnp.dot(both, U[...], preferred_element_type=F32)
    d_unit = student_scale * jnp.sum(rows, axis=0, keepdims=True)
    along = jnp.sum(unit32 * d_unit, axis=-1, keepdims=True)
    d_student = (d_unit - unit32 * along) / norm_s
    d16 = jnp.broadcast_to(d_student, (16, emb)).astype(BF16)
    cbuf[x] = lax.dot_general(d16, w2v[...], NT, preferred_element_type=F32)[:1] / tokens
    for d in range(1, nx):
        send(cbuf.at[x], cbuf.at[x], cs.at[d], cr.at[x], {"x": me.at_x(d)})

    log_q = log_probabilities(s_log)
    terms = jnp.where(diagonal, 0.0, prob_p * (log_p - log_q))
    loss_out[...] = jnp.sum(jnp.sum(terms, axis=1, keepdims=True), axis=0, keepdims=True) / count

    pre_arrives(3)
    pre_arrives(2)
    sum_v = jnp.zeros((tokens, LANES), F32)
    sum_p = jnp.zeros((tokens, LANES), F32)
    for d in (0, 1, 3, 2):
        xx = me.at_x(d)
        if d:
            arrive(cbuf.at[xx], cs.at[0], cr.at[xx], {"x": xx})
        for k in range(hid // LANES):
            t = slice(k * LANES, (k + 1) * LANES)
            dp = (sl[xx, :, t].astype(F32) * cbuf[xx, :, t]).astype(BF16)
            sl[xx, :, t] = dp
            dp = dp.astype(F32)
            sum_v += dp * xbuf[xx, :, emb + k * LANES : emb + (k + 1) * LANES]
            sum_p += dp * sb[xx, :, t].astype(F32)
    mean_g = jnp.sum(sum_v, axis=1, keepdims=True) / width
    mean_c = jnp.sum(sum_p, axis=1, keepdims=True) / width

    for d in range(1, nx):
        xx = me.at_x(d)
        for j, k in enumerate((0, 3, 1, 2)):
            q = lax.rem(color + k, 4)
            r = pl.ds(pl.multiple_of(q * quarter + (1 - c) * piece, 16), piece)
            arrive(wc.at[xx, r], wds.at[0, 0], wdr.at[j, d], {"core": 1 - c})

    step = 2 * LANES
    for j in range(cols // step):
        own = pl.ds(pl.multiple_of(x * cols + j * step, LANES), step)
        grad = lax.dot_general(sl[x], wv[own, :], NT, preferred_element_type=F32)
        for d in range(1, nx):
            xx = me.at_x(d)
            grad += lax.dot_general(
                sl[xx], wc[xx, j * step : (j + 1) * step, :], NT, preferred_element_type=F32
            )
        for h in range(2):
            k = 2 * j + h
            t = slice(k * LANES, (k + 1) * LANES)
            gt = grad[:, h * LANES : (h + 1) * LANES] * gain[:, own_columns(k)]
            out[0, :, t] = (rstdv[...] * (gt - mean_g - xh[:, t] * mean_c)).astype(BF16)
    for cp in waits:
        cp.wait_send()


def on_device(sizes, pooled, layer_norm_gain, w_first, w_second, teacher):
    images, tokens, width = pooled.shape
    hid = w_first.shape[1]
    emb = w_second.shape[1]
    ny, nz, nx = sizes["yh"] * sizes["yl"], sizes["z"], sizes["x"]
    count = 2 * ny * nz
    cols = width // nx
    dma = lambda *n: pltpu.SemaphoreType.DMA(n)
    gather = lambda: [dma(nz), dma(nz), dma(ny), dma(ny), dma(ny), dma(ny)]
    hbm, vmem = pl.BlockSpec(memory_space=pl.ANY), pl.BlockSpec(memory_space=pltpu.VMEM)
    grad, loss = pl.pallas_call(
        functools.partial(step_kernel, sizes),
        out_shape=(
            jax.ShapeDtypeStruct((images, tokens, cols), BF16),
            jax.ShapeDtypeStruct((1, 1), F32),
        ),
        in_specs=[hbm, vmem, hbm, hbm, vmem],
        out_specs=(vmem, vmem),
        scratch_shapes=[
            pltpu.VMEM((tokens, width), BF16),
            pltpu.VMEM((tokens + 16, width), BF16),
            pltpu.VMEM((width, hid), BF16),
            pltpu.VMEM((hid, emb), BF16),
            pltpu.VMEM((nx, cols, hid), BF16),
            pltpu.VMEM((tokens + 16, hid), F32),
            pltpu.VMEM((nx, tokens, hid), BF16),
            pltpu.VMEM((nx, tokens, hid), BF16),
            pltpu.VMEM((tokens, cols), F32),
            pltpu.VMEM((8, LANES), F32),
            pltpu.VMEM((tokens, LANES), F32),
            pltpu.VMEM((tokens, LANES), F32),
            pltpu.VMEM((nx, 1, emb + hid), F32),
            pltpu.VMEM((nx, 1, hid), F32),
            pltpu.VMEM((2, ny, nz, 8, LANES), BF16),
            pltpu.VMEM((2, ny, nz, 8, LANES), BF16),
            pltpu.VMEM((count * 8, LANES), F32),
            pltpu.VMEM((count, emb), BF16),
            pltpu.VMEM((count, emb), BF16),
            dma(2 + nx), dma(nx), dma(nx), dma(nx), dma(nx), dma(nx), dma(nx),
            *gather(), *gather(),
            dma(nx), dma(nx), dma(2, nx), dma(2, nx), dma(2, nx), dma(2, nx), dma(4, nx), dma(4, nx),
        ],
        compiler_params=pltpu.CompilerParams(collective_id=0, has_side_effects=True),
    )(pooled, layer_norm_gain.reshape(1, width), w_first, w_second, teacher)
    return loss[0, 0], grad


def solution(mesh):
    names = ("yh", "core", "yl", "z", "x")
    split = Mesh(mesh.devices.reshape(4, 2, 2, 12, mesh.shape["tensor"]), names)
    in_specs = (P(IMAGES, None, None), P(), P(None, "x"), P("x", None), P(IMAGES, None))
    out_specs = (P(), P(IMAGES, None, "x"))
    return jax.shard_map(
        functools.partial(on_device, dict(split.shape)),
        mesh=split, in_specs=in_specs, out_specs=out_specs, check_vma=False,
    )
```

```python
import functools

import jax
import jax.numpy as jnp
from jax import lax
from jax.experimental import pallas as pl
from jax.experimental.pallas import tpu as pltpu
from jax.sharding import Mesh
from jax.sharding import PartitionSpec as P

IMAGES = ("yh", "core", "yl", "z")
MESH = pl.DeviceIdType.MESH

student_scale = 10.0
teacher_scale = 20.0
masked_value = -1000000000.0
F32, BF16 = jnp.float32, jnp.bfloat16
NT = (((1,), (1,)), ((), ()))
LANES = 128
BLOCK = 64


def as_tile(row):
    return jnp.concatenate([row[:, k * 128 : (k + 1) * 128] for k in range(8)], axis=0)


def normal_cdf(v):
    return 0.5 * (1.0 + lax.erf(v * 0.7071067811865476))


class Place:
    def __init__(self, sizes):
        self.x, self.z, self.c = (lax.axis_index(a) for a in ("x", "z", "core"))
        self.nx, self.nz = sizes["x"], sizes["z"]
        self.nl = sizes["yl"]
        self.ny = sizes["yh"] * sizes["yl"]
        self.y = lax.axis_index("yh") * self.nl + lax.axis_index("yl")
        self.row = (self.c * self.ny + self.y) * self.nz + self.z

    def at_x(self, d):
        return lax.rem(self.x + d, self.nx)

    def at_y(self, d):
        return lax.rem(self.y + d, self.ny)

    def at_z(self, d):
        return lax.rem(self.z + d, self.nz)

    def to_y(self, yy):
        return {"yh": yy // self.nl, "yl": lax.rem(yy, self.nl)}


def remote(src, dst, ss, rs, where):
    return pltpu.make_async_remote_copy(
        src_ref=src, dst_ref=dst, send_sem=ss, recv_sem=rs, device_id=where, device_id_type=MESH
    )


def step_kernel(sizes, pooled, gain_hbm, w1, w2, tea_hbm, out, loss_out,
                gain, tea, xv, nv, wv, w2v, wc, pv, sb, sl, xh, acc, meanv, rstdv,
                xbuf, cbuf, ub, tb, wide, U, T,
                local, done, xs, xr, cs, cr, ps, pr,
                uzs, uzr, uys, uyr, ucs, ucr, tzs, tzr, tys, tyr, tcs, tcr,
                wxs, wxr, prs, prr, wzs, wzr, wys, wyr, wds, wdr):
    me = Place(sizes)
    x, y, z, c = me.x, me.y, me.z, me.c
    nx, ny, nz = me.nx, me.ny, me.nz
    count = 2 * ny * nz
    tokens, width = xv.shape
    hid = wv.shape[1]
    emb = w2v.shape[1]
    cols = width // nx
    tiles = width // LANES

    get_tea = pltpu.make_async_copy(tea_hbm, tea, local.at[2 + nx])
    get_tea.start()
    get_gain = pltpu.make_async_copy(gain_hbm, gain, local.at[3 + nx])
    get_gain.start()

    get_x = []
    for k in range(nx):
        t = pl.ds(k * cols, cols)
        get_x.append(pltpu.make_async_copy(pooled.at[0, :, t], xv.at[:, t], local.at[4 + nx + k]))
        get_x[-1].start()
    barrier = pltpu.get_barrier_semaphore()
    peers = (
        [{"x": me.at_x(d)} for d in range(1, nx)]
        + [{"z": me.at_z(d)} for d in range(1, nz)]
        + [me.to_y(me.at_y(d)) for d in range(1, ny)]
        + [{"core": 1 - c}]
    )
    for p in peers:
        pl.semaphore_signal(barrier, inc=1, device_id=p, device_id_type=MESH)

    get_w = []
    for k in range(nx):
        rows = pl.ds(k * cols, cols)
        get_w.append(pltpu.make_async_copy(w1.at[rows], wv.at[rows], local.at[1 + k]))
    get_w2 = pltpu.make_async_copy(w2, w2v, local.at[1 + nx])

    sent = []

    def send(src, dst, ss, rs, where):
        remote(src, dst, ss, rs, where).start()

    def arrive(ref, rs):
        remote(ref, ref, done.at[0], rs, {"core": 1 - c}).wait_recv()

    def left(ref, ss):
        sent.append(remote(ref, ref, ss, done.at[0], {"core": 1 - c}))

    ones = jnp.ones((cols, LANES), BF16)
    total = jnp.zeros((tokens, LANES), F32)
    for k in range(nx):
        get_x[k].wait()
        if k == nx - 1:
            for cp in get_w:
                cp.start()
            get_w2.start()
        total += jnp.dot(xv[:, k * cols : (k + 1) * cols], ones, preferred_element_type=F32)
    meanv[...] = total / width

    @pl.loop(0, tokens // BLOCK)
    def _(i):
        r = pl.ds(pl.multiple_of(i * BLOCK, BLOCK), BLOCK)
        m = meanv[r, :]
        squares = jnp.zeros((BLOCK, LANES), F32)
        for k in range(tiles):
            dev = xv[r, k * LANES : (k + 1) * LANES].astype(F32) - m
            squares += dev * dev
        var = jnp.sum(squares, axis=1, keepdims=True) / width
        rstdv[r, :] = jnp.broadcast_to(lax.rsqrt(var + 1e-05), (BLOCK, LANES))

    def z_send(buf, ss, rs):
        for d in range(1, nz):
            send(buf.at[c, y, z], buf.at[c, y, z], ss, rs, {"z": me.at_z(d)})
        left(buf.at[c, y, pl.ds(0, nz - 1)], ss)

    def z_wait(buf, rs):
        arrive(buf.at[c, y, pl.ds(0, nz - 1)], rs)

    def y_send(buf, ss, rs):
        for d in (4, 3, 5, 2, 6, 1, 7):
            yy = me.at_y(d)
            send(buf.at[c, y], buf.at[c, y], ss, rs(y), me.to_y(yy))
        left(buf.at[c, pl.ds(0, ny - 1)], ss)

    quarter = cols // 4
    piece = quarter // 2
    half = piece // 2
    color = lax.rem(2 * y + z, 4)

    def place(k, part=0, length=piece):
        q = lax.rem(color + k, 4)
        return pl.ds(pl.multiple_of(q * quarter + c * piece + part, 16), length)

    get_tea.wait()
    tvals = tea[...].astype(F32)
    tunit = tvals / jnp.sqrt(jnp.sum(tvals * tvals, axis=-1, keepdims=True) + 1e-06)
    tb[c, y, z] = as_tile(tunit).astype(BF16)
    get_gain.wait()
    g = gain[...]
    g_hi = g.astype(BF16)
    g_lo = (g - g_hi.astype(F32)).astype(BF16)
    sub16 = lax.broadcasted_iota(jnp.int32, (16, width), 0)
    nv[tokens:, :] = jnp.where(
        sub16 == 0, g_hi.astype(F32), jnp.where(sub16 == 1, g_lo.astype(F32), 0.0)
    ).astype(BF16)

    @pl.loop(0, tokens // BLOCK)
    def _(i):
        r = pl.ds(pl.multiple_of(i * BLOCK, BLOCK), BLOCK)
        m, s = meanv[r, :], rstdv[r, :]
        for k in range(tiles):
            t = slice(k * LANES, (k + 1) * LANES)
            nv[r, t] = ((xv[r, t].astype(F32) - m) * s * gain[:, t]).astype(BF16)

    pl.semaphore_wait(barrier, len(peers))

    def w_send(d):
        xx = me.at_x(d)
        start = pl.multiple_of(xx * cols + color * quarter + c * piece, 16)
        send(w1.at[pl.ds(start, piece)], wc.at[x, place(0)], wxs.at[0], wxr.at[x], {"x": xx})

    w_send(1)
    w_send(3)
    z_send(tb, tzs.at[0], tzr.at[0])

    for k in range(nx):
        get_w[k].wait()
        t = slice(k * cols, (k + 1) * cols)
        part = jnp.dot(nv[:, t], wv[t, :], preferred_element_type=F32)
        if k == 0:
            pv[...] = part
        else:
            pv[...] += part

    pool = []
    for k in range(hid // LANES):
        t = slice(k * LANES, (k + 1) * LANES)

        def body(i, total, t=t):
            r = pl.ds(pl.multiple_of(i * BLOCK, BLOCK), BLOCK)
            p = pv[r, t]
            sb[x, r, t] = p.astype(BF16)
            act = p * normal_cdf(p)
            for j in range(BLOCK // 8):
                total += act[j * 8 : (j + 1) * 8]
            return total

        total = lax.fori_loop(0, tokens // BLOCK, body, jnp.zeros((8, LANES), F32))
        pool.append(jnp.sum(total, axis=0, keepdims=True))
    pool = jnp.concatenate(pool, axis=1) / tokens
    get_w2.wait()
    pool16 = jnp.broadcast_to(pool, (16, hid)).astype(BF16)
    xbuf[x, :, :emb] = jnp.dot(pool16, w2v[...], preferred_element_type=F32)[:1]
    xbuf[x, :, emb:] = pv[tokens : tokens + 1, :] + pv[tokens + 1 : tokens + 2, :]

    for d in range(1, nx):
        send(xbuf.at[x], xbuf.at[x], xs.at[0], xr.at[0], {"x": me.at_x(d)})
    left(xbuf.at[pl.ds(0, nx - 1)], xs.at[0])
    w_send(2)
    for d in (1, 3):
        send(sb.at[x], sb.at[x], ps.at[0], pr.at[d], {"x": me.at_x(d)})
    left(wc.at[0, pl.ds(0, 3 * piece)], wxs.at[0])
    left(sb.at[pl.ds(0, 2)], ps.at[0])
    arrive(xbuf.at[pl.ds(0, nx - 1)], xr.at[0])
    student = xbuf[0, :, :emb]
    for k in range(1, nx):
        student = student + xbuf[k, :, :emb]
    norm_s = jnp.sqrt(jnp.sum(student * student, axis=-1, keepdims=True) + 1e-06)
    unit32 = student / norm_s
    ub[c, y, z] = as_tile(unit32).astype(BF16)
    z_send(ub, uzs.at[0], uzr.at[0])
    z_wait(tb, tzr.at[0])
    y_send(tb, tys.at[0], lambda yy: tyr.at[0])

    def w_along_y(d):
        xx = me.at_x(d)
        low, high = wc.at[xx, place(0, 0, half)], wc.at[xx, place(0, half, half)]
        send(low, low, wys.at[0], wyr.at[0, d], me.to_y(me.at_y(1)))
        send(high, high, wys.at[0], wyr.at[1, d], me.to_y(me.at_y(ny - 1)))

    for d in (1, 3, 2):
        xx = me.at_x(d)
        block = wc.at[xx, place(0)]
        arrive(block, wxr.at[xx])
        send(block, block, wzs.at[0], wzr.at[0, d], {"z": me.at_z(1)})
        send(block, block, wzs.at[0], wzr.at[1, d], {"z": me.at_z(nz - 1)})
        if d == 1:
            w_along_y(d)
        send(block, block, wds.at[0], wdr.at[0, d], {"core": 1 - c})

    def own_columns(k):
        return pl.ds(pl.multiple_of(x * cols + k * LANES, LANES), LANES)

    for k in range(cols // LANES):
        t = slice(k * LANES, (k + 1) * LANES)
        xh[:, t] = (xv[:, own_columns(k)].astype(F32) - meanv[...]) * rstdv[...]

    def slope_of(xx):
        for k in range(hid // LANES):
            t = slice(k * LANES, (k + 1) * LANES)

            @pl.loop(0, tokens // BLOCK)
            def _(i, t=t):
                r = pl.ds(pl.multiple_of(i * BLOCK, BLOCK), BLOCK)
                p = sb[xx, r, t].astype(F32)
                s = normal_cdf(p) + p * jnp.exp(-0.5 * p * p) * 0.3989422804014327
                sl[xx, r, t] = s.astype(BF16)

    slope_of(x)
    z_wait(ub, uzr.at[0])
    y_send(ub, uys.at[0], lambda yy: uyr.at[yy])
    w_along_y(3)
    w_along_y(2)

    def assemble(buf, dst):
        wide[...] = buf[...].astype(F32).reshape(count * 8, LANES)
        for s in range(8):
            dst[:, s * LANES : (s + 1) * LANES] = wide[pl.ds(s, count, stride=8), :].astype(BF16)

    down = lax.broadcasted_iota(jnp.int32, (count, count), 0)
    across = lax.broadcasted_iota(jnp.int32, (count, count), 1)
    diagonal = down == across
    lane = lax.broadcasted_iota(jnp.int32, (1, count), 1)

    def similarity(mat, scale):
        a = mat[...]
        s = lax.dot_general(a, a, NT, preferred_element_type=F32)
        s = jnp.where(diagonal, masked_value, scale * s)
        topr = jnp.max(s, axis=0, keepdims=True)
        lse_r = topr + jnp.log(jnp.sum(jnp.exp(s - topr), axis=0, keepdims=True))
        own = jnp.sum(jnp.where(down == me.row, s, 0.0), axis=0, keepdims=True)
        lse_own = jnp.sum(jnp.where(lane == me.row, lse_r, 0.0), axis=1, keepdims=True)
        return s, jnp.exp(own - lse_own), jnp.exp(own - lse_r)

    def log_probabilities(s):
        top = jnp.max(s, axis=1, keepdims=True)
        return s - (top + jnp.log(jnp.sum(jnp.exp(s - top), axis=1, keepdims=True)))

    upper, lower = pl.ds(0, tokens // 2), pl.ds(tokens // 2, tokens // 2)
    after, before, far = me.at_x(1), me.at_x(3), me.at_x(2)
    arrive(sb.at[before], pr.at[1])
    arrive(sb.at[after], pr.at[3])
    send(sb.at[before, upper], sb.at[before, upper], prs.at[0], prr.at[0], {"x": after})
    send(sb.at[after, lower], sb.at[after, lower], prs.at[0], prr.at[1], {"x": before})
    slope_of(before)
    slope_of(after)
    arrive(tb.at[c, pl.ds(0, ny - 1)], tyr.at[0])
    send(tb.at[c], tb.at[c], tcs.at[0], tcr.at[0], {"core": 1 - c})
    left(tb.at[c], tcs.at[0])
    for d in (0, 1, 7, 2, 6, 3, 5, 4):
        yy = me.at_y(d)
        if d:
            arrive(ub.at[c, yy], uyr.at[yy])
        send(ub.at[c, yy], ub.at[c, yy], ucs.at[0], ucr.at[0], {"core": 1 - c})
    left(ub.at[c], ucs.at[0])

    arrive(tb.at[1 - c], tcr.at[0])
    assemble(tb, T)
    t_log, p_row, p_col = similarity(T, teacher_scale)
    log_p = log_probabilities(t_log)
    prob_p = jnp.exp(log_p)

    def w_across(d):
        xx = me.at_x(d)
        w_minus, w_plus = wc.at[xx, place(3)], wc.at[xx, place(1)]
        arrive(w_minus, wzr.at[0, d])
        send(w_minus, w_minus, wds.at[0], wdr.at[1, d], {"core": 1 - c})
        arrive(w_plus, wzr.at[1, d])
        send(w_plus, w_plus, wds.at[0], wdr.at[2, d], {"core": 1 - c})
        arrive(wc.at[xx, place(2, 0, half)], wyr.at[0, d])
        arrive(wc.at[xx, place(2, half, half)], wyr.at[1, d])
        other = wc.at[xx, place(2)]
        send(other, other, wds.at[0], wdr.at[3, d], {"core": 1 - c})

    w_across(1)
    arrive(ub.at[1 - c], ucr.at[0])
    assemble(ub, U)
    s_log, q_row, q_col = similarity(U, student_scale)
    sub = lax.broadcasted_iota(jnp.int32, (16, count), 0)
    d_row = (q_row - p_row) / count
    d_col = (q_col - p_col) / count
    both = jnp.where(sub == 0, d_row, jnp.where(sub == 1, d_col, 0.0)).astype(BF16)
    rows = jnp.dot(both, U[...], preferred_element_type=F32)
    d_unit = student_scale * jnp.sum(rows, axis=0, keepdims=True)
    along = jnp.sum(unit32 * d_unit, axis=-1, keepdims=True)
    d_student = (d_unit - unit32 * along) / norm_s
    d16 = jnp.broadcast_to(d_student, (16, emb)).astype(BF16)
    cbuf[x] = lax.dot_general(d16, w2v[...], NT, preferred_element_type=F32)[:1] / tokens
    for d in range(1, nx):
        send(cbuf.at[x], cbuf.at[x], cs.at[0], cr.at[x], {"x": me.at_x(d)})
    left(cbuf.at[pl.ds(0, nx - 1)], cs.at[0])

    sums = [jnp.zeros((tokens, LANES), F32), jnp.zeros((tokens, LANES), F32)]

    def scale_slope(xx):
        for k in range(hid // LANES):
            t = slice(k * LANES, (k + 1) * LANES)
            dp = (sl[xx, :, t].astype(F32) * cbuf[xx, :, t]).astype(BF16)
            sl[xx, :, t] = dp
            dp = dp.astype(F32)
            sums[0] += dp * xbuf[xx, :, emb + k * LANES : emb + (k + 1) * LANES]
            sums[1] += dp * sb[xx, :, t].astype(F32)

    w_across(3)
    w_across(2)
    scale_slope(x)
    step = 2 * LANES
    for j in range(cols // step):
        own = pl.ds(pl.multiple_of(x * cols + j * step, LANES), step)
        acc[:, j * step : (j + 1) * step] = lax.dot_general(
            sl[x], wv[own, :], NT, preferred_element_type=F32
        )
    arrive(sb.at[far, upper], prr.at[0])
    arrive(sb.at[far, lower], prr.at[1])
    slope_of(far)
    log_q = log_probabilities(s_log)
    terms = jnp.where(diagonal, 0.0, prob_p * (log_p - log_q))
    loss_out[...] = jnp.sum(jnp.sum(terms, axis=1, keepdims=True), axis=0, keepdims=True) / count
    for d in (1, 3, 2):
        xx = me.at_x(d)
        arrive(cbuf.at[xx], cr.at[xx])
        scale_slope(xx)
        for j, k in enumerate((0, 3, 1, 2)):
            q = lax.rem(color + k, 4)
            r = pl.ds(pl.multiple_of(q * quarter + (1 - c) * piece, 16), piece)
            arrive(wc.at[xx, r], wdr.at[j, d])
        if d != 2:
            for j in range(cols // step):
                span = slice(j * step, (j + 1) * step)
                acc[:, span] += lax.dot_general(sl[xx], wc[xx, span, :], NT, preferred_element_type=F32)
    mean_g = jnp.sum(sums[0], axis=1, keepdims=True) / width
    mean_c = jnp.sum(sums[1], axis=1, keepdims=True) / width

    for j in range(cols // step):
        span = slice(j * step, (j + 1) * step)
        grad = acc[:, span] + lax.dot_general(sl[far], wc[far, span, :], NT, preferred_element_type=F32)
        for h in range(2):
            k = 2 * j + h
            t = slice(k * LANES, (k + 1) * LANES)
            gt = grad[:, h * LANES : (h + 1) * LANES] * gain[:, own_columns(k)]
            out[0, :, t] = (rstdv[...] * (gt - mean_g - xh[:, t] * mean_c)).astype(BF16)
    left(sb.at[0], prs.at[0])
    left(wc.at[0, pl.ds(0, 6 * piece)], wzs.at[0])
    left(wc.at[0, pl.ds(0, 6 * half)], wys.at[0])
    left(wc.at[pl.ds(0, 3), pl.ds(0, 4 * piece)], wds.at[0])
    for cp in sent:
        cp.wait_send()


def store_kernel(grad, loss, grad_out, loss_out, sem):
    put = pltpu.make_async_copy(grad, grad_out, sem)
    put.start()
    loss_out[...] = loss[...]
    put.wait()


def on_device(sizes, pooled, layer_norm_gain, w_first, w_second, teacher):
    images, tokens, width = pooled.shape
    hid = w_first.shape[1]
    emb = w_second.shape[1]
    ny, nz, nx = sizes["yh"] * sizes["yl"], sizes["z"], sizes["x"]
    count = 2 * ny * nz
    cols = width // nx
    dma = lambda *n: pltpu.SemaphoreType.DMA(n)
    hbm, vmem = pl.BlockSpec(memory_space=pltpu.HBM), pl.BlockSpec(memory_space=pltpu.VMEM)
    grad, loss = pl.pallas_call(
        functools.partial(step_kernel, sizes),
        out_shape=(
            pltpu.VMEM((images, tokens, cols), BF16),
            pltpu.VMEM((1, 1), F32),
        ),
        in_specs=[hbm] * 5,
        out_specs=(vmem, vmem),
        scratch_shapes=[
            pltpu.VMEM((1, width), F32),
            pltpu.VMEM((1, emb), BF16),
            pltpu.VMEM((tokens, width), BF16),
            pltpu.VMEM((tokens + 16, width), BF16),
            pltpu.VMEM((width, hid), BF16),
            pltpu.VMEM((hid, emb), BF16),
            pltpu.VMEM((nx, cols, hid), BF16),
            pltpu.VMEM((tokens + 16, hid), F32),
            pltpu.VMEM((nx, tokens, hid), BF16),
            pltpu.VMEM((nx, tokens, hid), BF16),
            pltpu.VMEM((tokens, cols), F32),
            pltpu.VMEM((tokens, cols), F32),
            pltpu.VMEM((tokens, LANES), F32),
            pltpu.VMEM((tokens, LANES), F32),
            pltpu.VMEM((nx, 1, emb + hid), F32),
            pltpu.VMEM((nx, 1, hid), F32),
            pltpu.VMEM((2, ny, nz, 8, LANES), BF16),
            pltpu.VMEM((2, ny, nz, 8, LANES), BF16),
            pltpu.VMEM((count * 8, LANES), F32),
            pltpu.VMEM((count, emb), BF16),
            pltpu.VMEM((count, emb), BF16),
            dma(4 + 2 * nx), dma(1), dma(1), dma(1), dma(1), dma(nx), dma(1), dma(nx),
            dma(1), dma(1), dma(1), dma(ny), dma(1), dma(1),
            dma(1), dma(1), dma(1), dma(1), dma(1), dma(1),
            dma(1), dma(nx), dma(1), dma(2), dma(1), dma(2, nx), dma(1), dma(2, nx), dma(1), dma(4, nx),
        ],
        compiler_params=pltpu.CompilerParams(collective_id=0, has_side_effects=True, vmem_limit_bytes=48 * 2**20),
    )(*(pltpu.with_memory_space_constraint(a, pltpu.HBM) for a in (pooled, layer_norm_gain.reshape(1, width), w_first, w_second, teacher)))
    grad, loss = pl.pallas_call(
        store_kernel,
        out_shape=(jax.ShapeDtypeStruct((images, tokens, cols), BF16), jax.ShapeDtypeStruct((1, 1), F32)),
        in_specs=[vmem, vmem],
        out_specs=(hbm, vmem),
        scratch_shapes=[pltpu.SemaphoreType.DMA],
        compiler_params=pltpu.CompilerParams(vmem_limit_bytes=2**20),
    )(pltpu.with_memory_space_constraint(grad, pltpu.VMEM), pltpu.with_memory_space_constraint(loss, pltpu.VMEM))
    return loss[0, 0], grad


def solution(mesh):
    names = ("yh", "core", "yl", "z", "x")
    split = Mesh(mesh.devices.reshape(4, 2, 2, 12, mesh.shape["tensor"]), names)
    in_specs = (P(IMAGES, None, None), P(), P(None, "x"), P("x", None), P(IMAGES, None))
    out_specs = (P(), P(IMAGES, None, "x"))
    return jax.shard_map(
        functools.partial(on_device, dict(split.shape)),
        mesh=split, in_specs=in_specs, out_specs=out_specs, check_vma=False,
    )
```

```python
import functools

import jax
import jax.numpy as jnp
from jax import lax
from jax.experimental import pallas as pl
from jax.experimental.pallas import tpu as pltpu
from jax.sharding import Mesh
from jax.sharding import PartitionSpec as P

IMAGES = ("yh", "core", "yl", "z")
MESH = pl.DeviceIdType.MESH

student_scale = 10.0
teacher_scale = 20.0
masked_value = -1000000000.0
F32, BF16 = jnp.float32, jnp.bfloat16
NT = (((1,), (1,)), ((), ()))
LANES = 128
BLOCK = 64


def as_tile(row):
    return jnp.concatenate([row[:, k * 128 : (k + 1) * 128] for k in range(8)], axis=0)


def normal_cdf(v):
    return 0.5 * (1.0 + lax.erf(v * 0.7071067811865476))


class Place:
    def __init__(self, sizes):
        self.x, self.z, self.c = (lax.axis_index(a) for a in ("x", "z", "core"))
        self.nx, self.nz = sizes["x"], sizes["z"]
        self.nl = sizes["yl"]
        self.ny = sizes["yh"] * sizes["yl"]
        self.y = lax.axis_index("yh") * self.nl + lax.axis_index("yl")
        self.row = (self.c * self.ny + self.y) * self.nz + self.z

    def at_x(self, d):
        return lax.rem(self.x + d, self.nx)

    def at_y(self, d):
        return lax.rem(self.y + d, self.ny)

    def at_z(self, d):
        return lax.rem(self.z + d, self.nz)

    def to_y(self, yy):
        return {"yh": yy // self.nl, "yl": lax.rem(yy, self.nl)}


def remote(src, dst, ss, rs, where):
    return pltpu.make_async_remote_copy(
        src_ref=src, dst_ref=dst, send_sem=ss, recv_sem=rs, device_id=where, device_id_type=MESH
    )


def step_kernel(sizes, pooled, gain_hbm, w1, w2, tea_hbm, out, loss_out,
                gain, tea, xv, nv, wv, w2v, wc, pv, sb, sl, xh, acc, meanv, rstdv,
                xbuf, cbuf, ub, tb, wide, U, T,
                local, done, xs, xr, cs, cr, ps, pr,
                uzs, uzr, uys, uyr, ucs, ucr, tzs, tzr, tys, tyr, tcs, tcr,
                wxs, wxr, prs, prr, wzs, wzr, wys, wyr, wds, wdr):
    me = Place(sizes)
    x, y, z, c = me.x, me.y, me.z, me.c
    nx, ny, nz = me.nx, me.ny, me.nz
    count = 2 * ny * nz
    tokens, width = xv.shape
    hid = wv.shape[1]
    emb = w2v.shape[1]
    cols = width // nx
    tiles = width // LANES

    get_tea = pltpu.make_async_copy(tea_hbm, tea, local.at[2 + nx])
    get_tea.start()
    get_gain = pltpu.make_async_copy(gain_hbm, gain, local.at[3 + nx])
    get_gain.start()

    get_x = []
    for k in range(tokens // BLOCK):
        t = pl.ds(k * BLOCK, BLOCK)
        get_x.append(pltpu.make_async_copy(pooled.at[0, t], xv.at[t], local.at[4 + nx + k]))
        get_x[-1].start()
    barrier = pltpu.get_barrier_semaphore()
    peers = (
        [{"x": me.at_x(d)} for d in range(1, nx)]
        + [{"z": me.at_z(d)} for d in range(1, nz)]
        + [me.to_y(me.at_y(d)) for d in range(1, ny)]
        + [{"core": 1 - c}]
    )
    for p in peers:
        pl.semaphore_signal(barrier, inc=1, device_id=p, device_id_type=MESH)

    get_w = []
    for k in range(nx):
        rows = pl.ds(k * cols, cols)
        get_w.append(pltpu.make_async_copy(w1.at[rows], wv.at[rows], local.at[1 + k]))
    get_w2 = pltpu.make_async_copy(w2, w2v, local.at[1 + nx])

    sent = []

    def send(src, dst, ss, rs, where):
        remote(src, dst, ss, rs, where).start()

    def arrive(ref, rs):
        remote(ref, ref, done.at[0], rs, {"core": 1 - c}).wait_recv()

    def left(ref, ss):
        sent.append(remote(ref, ref, ss, done.at[0], {"core": 1 - c}))

    get_gain.wait()
    for i in range(tokens // BLOCK):
        get_x[i].wait()
        if i == 1:
            for cp in get_w:
                cp.start()
            get_w2.start()
        r = slice(i * BLOCK, (i + 1) * BLOCK)
        total = jnp.zeros((BLOCK, LANES), F32)
        for k in range(tiles):
            total += xv[r, k * LANES : (k + 1) * LANES].astype(F32)
        m = jnp.broadcast_to(jnp.sum(total, axis=1, keepdims=True) / width, (BLOCK, LANES))
        squares = jnp.zeros((BLOCK, LANES), F32)
        for k in range(tiles):
            dev = xv[r, k * LANES : (k + 1) * LANES].astype(F32) - m
            squares += dev * dev
        var = jnp.sum(squares, axis=1, keepdims=True) / width
        rs = jnp.broadcast_to(lax.rsqrt(var + 1e-05), (BLOCK, LANES))
        meanv[r, :] = m
        rstdv[r, :] = rs
        for k in range(tiles):
            t = slice(k * LANES, (k + 1) * LANES)
            nv[r, t] = ((xv[r, t].astype(F32) - m) * rs * gain[:, t]).astype(BF16)

    def z_send(buf, ss, rs):
        for d in range(1, nz):
            send(buf.at[c, y, z], buf.at[c, y, z], ss, rs, {"z": me.at_z(d)})
        left(buf.at[c, y, pl.ds(0, nz - 1)], ss)

    def z_wait(buf, rs):
        arrive(buf.at[c, y, pl.ds(0, nz - 1)], rs)

    def y_send(buf, ss, rs):
        for d in (4, 3, 5, 2, 6, 1, 7):
            yy = me.at_y(d)
            send(buf.at[c, y], buf.at[c, y], ss, rs(y), me.to_y(yy))
        left(buf.at[c, pl.ds(0, ny - 1)], ss)

    quarter = cols // 4
    piece = quarter // 2
    half = piece // 2
    color = lax.rem(2 * y + z, 4)

    def place(k, part=0, length=piece):
        q = lax.rem(color + k, 4)
        return pl.ds(pl.multiple_of(q * quarter + c * piece + part, 16), length)


    first = 48

    def w_send(d, at, rows):
        xx = me.at_x(d)
        start = pl.multiple_of(xx * cols + color * quarter + c * piece + at, 16)
        send(w1.at[pl.ds(start, rows)], wc.at[x, place(0, at, rows)], wxs.at[0], wxr.at[x], {"x": xx})

    get_tea.wait()
    tvals = tea[...].astype(F32)
    tunit = tvals / jnp.sqrt(jnp.sum(tvals * tvals, axis=-1, keepdims=True) + 1e-06)
    tb[c, y, z] = as_tile(tunit).astype(BF16)
    g = gain[...]
    g_hi = g.astype(BF16)
    g_lo = (g - g_hi.astype(F32)).astype(BF16)
    sub16 = lax.broadcasted_iota(jnp.int32, (16, width), 0)
    nv[tokens:, :] = jnp.where(
        sub16 == 0, g_hi.astype(F32), jnp.where(sub16 == 1, g_lo.astype(F32), 0.0)
    ).astype(BF16)

    for k in range(nx):
        get_w[k].wait()
        if k == nx - 1:
            pl.semaphore_wait(barrier, len(peers))
            w_send(1, 0, first)
            w_send(3, 0, first)
            z_send(tb, tzs.at[0], tzr.at[0])
        t = slice(k * cols, (k + 1) * cols)
        part = jnp.dot(nv[:, t], wv[t, :], preferred_element_type=F32)
        if k == 0:
            pv[...] = part
        else:
            pv[...] += part

    pool = []
    for k in range(hid // LANES):
        t = slice(k * LANES, (k + 1) * LANES)

        def body(i, total, t=t):
            r = pl.ds(pl.multiple_of(i * BLOCK, BLOCK), BLOCK)
            p = pv[r, t]
            sb[x, r, t] = p.astype(BF16)
            act = p * normal_cdf(p)
            for j in range(BLOCK // 8):
                total += act[j * 8 : (j + 1) * 8]
            return total

        total = lax.fori_loop(0, tokens // BLOCK, body, jnp.zeros((8, LANES), F32))
        pool.append(jnp.sum(total, axis=0, keepdims=True))
    pool = jnp.concatenate(pool, axis=1) / tokens
    get_w2.wait()
    pool16 = jnp.broadcast_to(pool, (16, hid)).astype(BF16)
    xbuf[x, :, :emb] = jnp.dot(pool16, w2v[...], preferred_element_type=F32)[:1]
    xbuf[x, :, emb:] = pv[tokens : tokens + 1, :] + pv[tokens + 1 : tokens + 2, :]

    for d in range(1, nx):
        send(xbuf.at[x], xbuf.at[x], xs.at[0], xr.at[0], {"x": me.at_x(d)})
    left(xbuf.at[pl.ds(0, nx - 1)], xs.at[0])
    w_send(1, first, piece - first)
    w_send(3, first, piece - first)
    w_send(2, 0, piece)
    for d in (1, 3):
        send(sb.at[x], sb.at[x], ps.at[0], pr.at[d], {"x": me.at_x(d)})
    left(wc.at[0, pl.ds(0, 3 * piece)], wxs.at[0])
    left(sb.at[pl.ds(0, 2)], ps.at[0])
    arrive(xbuf.at[pl.ds(0, nx - 1)], xr.at[0])
    student = xbuf[0, :, :emb]
    for k in range(1, nx):
        student = student + xbuf[k, :, :emb]
    norm_s = jnp.sqrt(jnp.sum(student * student, axis=-1, keepdims=True) + 1e-06)
    unit32 = student / norm_s
    ub[c, y, z] = as_tile(unit32).astype(BF16)
    z_send(ub, uzs.at[0], uzr.at[0])
    z_wait(tb, tzr.at[0])
    y_send(tb, tys.at[0], lambda yy: tyr.at[0])

    def w_along_y(d):
        xx = me.at_x(d)
        low, high = wc.at[xx, place(0, 0, half)], wc.at[xx, place(0, half, half)]
        send(low, low, wys.at[0], wyr.at[d], me.to_y(me.at_y(1)))
        send(high, high, wys.at[0], wyr.at[d], me.to_y(me.at_y(ny - 1)))

    def w_from_x(d):
        xx = me.at_x(d)
        block = wc.at[xx, place(0)]
        arrive(block, wxr.at[xx])
        send(block, block, wzs.at[0], wzr.at[d], {"z": me.at_z(1)})
        send(block, block, wzs.at[0], wzr.at[d], {"z": me.at_z(nz - 1)})
        send(block, block, wds.at[0], wdr.at[d], {"core": 1 - c})

    w_from_x(1)
    w_along_y(1)
    w_from_x(3)

    def own_columns(k):
        return pl.ds(pl.multiple_of(x * cols + k * LANES, LANES), LANES)

    for k in range(cols // LANES):
        t = slice(k * LANES, (k + 1) * LANES)
        xh[:, t] = (xv[:, own_columns(k)].astype(F32) - meanv[...]) * rstdv[...]

    def slope_of(xx):
        for k in range(hid // LANES):
            t = slice(k * LANES, (k + 1) * LANES)

            @pl.loop(0, tokens // BLOCK)
            def _(i, t=t):
                r = pl.ds(pl.multiple_of(i * BLOCK, BLOCK), BLOCK)
                p = sb[xx, r, t].astype(F32)
                s = normal_cdf(p) + p * jnp.exp(-0.5 * p * p) * 0.3989422804014327
                sl[xx, r, t] = s.astype(BF16)

    slope_of(x)
    z_wait(ub, uzr.at[0])
    y_send(ub, uys.at[0], lambda yy: uyr.at[yy])
    w_from_x(2)
    w_along_y(3)
    w_along_y(2)

    def assemble(buf, dst):
        wide[...] = buf[...].astype(F32).reshape(count * 8, LANES)
        for s in range(8):
            dst[:, s * LANES : (s + 1) * LANES] = wide[pl.ds(s, count, stride=8), :].astype(BF16)

    down = lax.broadcasted_iota(jnp.int32, (count, count), 0)
    across = lax.broadcasted_iota(jnp.int32, (count, count), 1)
    diagonal = down == across
    lane = lax.broadcasted_iota(jnp.int32, (1, count), 1)

    def similarity(mat, scale):
        a = mat[...]
        s = lax.dot_general(a, a, NT, preferred_element_type=F32)
        s = jnp.where(diagonal, masked_value, scale * s)
        topr = jnp.max(s, axis=0, keepdims=True)
        lse_r = topr + jnp.log(jnp.sum(jnp.exp(s - topr), axis=0, keepdims=True))
        own = jnp.sum(jnp.where(down == me.row, s, 0.0), axis=0, keepdims=True)
        lse_own = jnp.sum(jnp.where(lane == me.row, lse_r, 0.0), axis=1, keepdims=True)
        return s, jnp.exp(own - lse_own), jnp.exp(own - lse_r)

    def log_probabilities(s):
        top = jnp.max(s, axis=1, keepdims=True)
        return s - (top + jnp.log(jnp.sum(jnp.exp(s - top), axis=1, keepdims=True)))

    arrive(tb.at[c, pl.ds(0, ny - 1)], tyr.at[0])
    send(tb.at[c], tb.at[c], tcs.at[0], tcr.at[0], {"core": 1 - c})
    left(tb.at[c], tcs.at[0])
    for d in (0, 1, 7, 2, 6, 3, 5, 4):
        yy = me.at_y(d)
        if d:
            arrive(ub.at[c, yy], uyr.at[yy])
        send(ub.at[c, yy], ub.at[c, yy], ucs.at[0], ucr.at[0], {"core": 1 - c})
    left(ub.at[c], ucs.at[0])

    arrive(tb.at[1 - c], tcr.at[0])
    assemble(tb, T)
    t_log, p_row, p_col = similarity(T, teacher_scale)
    log_p = log_probabilities(t_log)
    prob_p = jnp.exp(log_p)

    def w_across(d):
        xx = me.at_x(d)
        arrive(wc.at[xx, pl.ds(0, 2 * piece)], wzr.at[d])
        arrive(wc.at[xx, pl.ds(0, piece)], wyr.at[d])
        for k in (3, 1, 2):
            share = wc.at[xx, place(k)]
            send(share, share, wds.at[0], wdr.at[d], {"core": 1 - c})

    upper, lower = pl.ds(0, tokens // 2), pl.ds(tokens // 2, tokens // 2)
    after, before, far = me.at_x(1), me.at_x(3), me.at_x(2)
    arrive(sb.at[before], pr.at[1])
    arrive(sb.at[after], pr.at[3])
    send(sb.at[before, upper], sb.at[before, upper], prs.at[0], prr.at[0], {"x": after})
    send(sb.at[after, lower], sb.at[after, lower], prs.at[0], prr.at[1], {"x": before})
    w_across(1)
    arrive(ub.at[1 - c], ucr.at[0])
    assemble(ub, U)
    s_log, q_row, q_col = similarity(U, student_scale)
    sub = lax.broadcasted_iota(jnp.int32, (16, count), 0)
    d_row = (q_row - p_row) / count
    d_col = (q_col - p_col) / count
    both = jnp.where(sub == 0, d_row, jnp.where(sub == 1, d_col, 0.0)).astype(BF16)
    rows = jnp.dot(both, U[...], preferred_element_type=F32)
    d_unit = student_scale * jnp.sum(rows, axis=0, keepdims=True)
    along = jnp.sum(unit32 * d_unit, axis=-1, keepdims=True)
    d_student = (d_unit - unit32 * along) / norm_s
    d16 = jnp.broadcast_to(d_student, (16, emb)).astype(BF16)
    cbuf[x] = lax.dot_general(d16, w2v[...], NT, preferred_element_type=F32)[:1] / tokens
    for d in range(1, nx):
        send(cbuf.at[x], cbuf.at[x], cs.at[0], cr.at[x], {"x": me.at_x(d)})
    left(cbuf.at[pl.ds(0, nx - 1)], cs.at[0])

    sums = [jnp.zeros((tokens, LANES), F32), jnp.zeros((tokens, LANES), F32)]

    def scale_slope(xx):
        for k in range(hid // LANES):
            t = slice(k * LANES, (k + 1) * LANES)
            dp = (sl[xx, :, t].astype(F32) * cbuf[xx, :, t]).astype(BF16)
            sl[xx, :, t] = dp
            dp = dp.astype(F32)
            sums[0] += dp * xbuf[xx, :, emb + k * LANES : emb + (k + 1) * LANES]
            sums[1] += dp * sb[xx, :, t].astype(F32)

    w_across(3)
    scale_slope(x)
    step = 2 * LANES
    for j in range(cols // step):
        own = pl.ds(pl.multiple_of(x * cols + j * step, LANES), step)
        acc[:, j * step : (j + 1) * step] = lax.dot_general(
            sl[x], wv[own, :], NT, preferred_element_type=F32
        )
    w_across(2)
    slope_of(before)
    slope_of(after)
    log_q = log_probabilities(s_log)
    terms = jnp.where(diagonal, 0.0, prob_p * (log_p - log_q))
    loss_out[...] = jnp.sum(jnp.sum(terms, axis=1, keepdims=True), axis=0, keepdims=True) / count
    for d in (1, 3, 2):
        xx = me.at_x(d)
        if d == 2:
            arrive(sb.at[far, upper], prr.at[0])
            arrive(sb.at[far, lower], prr.at[1])
            slope_of(far)
        arrive(cbuf.at[xx], cr.at[xx])
        scale_slope(xx)
        arrive(wc.at[xx, pl.ds(0, 4 * piece)], wdr.at[d])
        if d != 2:
            for j in range(cols // step):
                span = slice(j * step, (j + 1) * step)
                acc[:, span] += lax.dot_general(sl[xx], wc[xx, span, :], NT, preferred_element_type=F32)
    mean_g = jnp.sum(sums[0], axis=1, keepdims=True) / width
    mean_c = jnp.sum(sums[1], axis=1, keepdims=True) / width

    for j in range(cols // step):
        span = slice(j * step, (j + 1) * step)
        grad = acc[:, span] + lax.dot_general(sl[far], wc[far, span, :], NT, preferred_element_type=F32)
        for h in range(2):
            k = 2 * j + h
            t = slice(k * LANES, (k + 1) * LANES)
            gt = grad[:, h * LANES : (h + 1) * LANES] * gain[:, own_columns(k)]
            out[0, :, t] = (rstdv[...] * (gt - mean_g - xh[:, t] * mean_c)).astype(BF16)
    left(sb.at[0], prs.at[0])
    left(wc.at[0, pl.ds(0, 6 * piece)], wzs.at[0])
    left(wc.at[0, pl.ds(0, 6 * half)], wys.at[0])
    left(wc.at[pl.ds(0, 3), pl.ds(0, 4 * piece)], wds.at[0])
    for cp in sent:
        cp.wait_send()


def store_kernel(grad, loss, grad_out, loss_out, sem):
    puts = [
        pltpu.make_async_copy(grad, grad_out, sem.at[0]),
        pltpu.make_async_copy(loss, loss_out, sem.at[1]),
    ]
    for put in puts:
        put.start()
    for put in puts:
        put.wait()


def on_device(sizes, pooled, layer_norm_gain, w_first, w_second, teacher):
    images, tokens, width = pooled.shape
    hid = w_first.shape[1]
    emb = w_second.shape[1]
    ny, nz, nx = sizes["yh"] * sizes["yl"], sizes["z"], sizes["x"]
    count = 2 * ny * nz
    cols = width // nx
    dma = lambda *n: pltpu.SemaphoreType.DMA(n)
    hbm, vmem = pl.BlockSpec(memory_space=pltpu.HBM), pl.BlockSpec(memory_space=pltpu.VMEM)
    grad, loss = pl.pallas_call(
        functools.partial(step_kernel, sizes),
        out_shape=(
            pltpu.VMEM((images, tokens, cols), BF16),
            pltpu.VMEM((1, 1), F32),
        ),
        in_specs=[hbm] * 5,
        out_specs=(vmem, vmem),
        scratch_shapes=[
            pltpu.VMEM((1, width), F32),
            pltpu.VMEM((1, emb), BF16),
            pltpu.VMEM((tokens, width), BF16),
            pltpu.VMEM((tokens + 16, width), BF16),
            pltpu.VMEM((width, hid), BF16),
            pltpu.VMEM((hid, emb), BF16),
            pltpu.VMEM((nx, cols, hid), BF16),
            pltpu.VMEM((tokens + 16, hid), F32),
            pltpu.VMEM((nx, tokens, hid), BF16),
            pltpu.VMEM((nx, tokens, hid), BF16),
            pltpu.VMEM((tokens, cols), F32),
            pltpu.VMEM((tokens, cols), F32),
            pltpu.VMEM((tokens, LANES), F32),
            pltpu.VMEM((tokens, LANES), F32),
            pltpu.VMEM((nx, 1, emb + hid), F32),
            pltpu.VMEM((nx, 1, hid), F32),
            pltpu.VMEM((2, ny, nz, 8, LANES), BF16),
            pltpu.VMEM((2, ny, nz, 8, LANES), BF16),
            pltpu.VMEM((count * 8, LANES), F32),
            pltpu.VMEM((count, emb), BF16),
            pltpu.VMEM((count, emb), BF16),
            dma(4 + 2 * nx), dma(1), dma(1), dma(1), dma(1), dma(nx), dma(1), dma(nx),
            dma(1), dma(1), dma(1), dma(ny), dma(1), dma(1),
            dma(1), dma(1), dma(1), dma(1), dma(1), dma(1),
            dma(1), dma(nx), dma(1), dma(2), dma(1), dma(nx), dma(1), dma(nx), dma(1), dma(nx),
        ],
        compiler_params=pltpu.CompilerParams(collective_id=0, has_side_effects=True, vmem_limit_bytes=48 * 2**20),
    )(*(pltpu.with_memory_space_constraint(a, pltpu.HBM) for a in (pooled, layer_norm_gain.reshape(1, width), w_first, w_second, teacher)))
    grad, loss = pl.pallas_call(
        store_kernel,
        out_shape=(jax.ShapeDtypeStruct((images, tokens, cols), BF16), jax.ShapeDtypeStruct((1, 1), F32)),
        in_specs=[vmem, vmem],
        out_specs=(hbm, hbm),
        scratch_shapes=[dma(2)],
        compiler_params=pltpu.CompilerParams(vmem_limit_bytes=2**20),
    )(pltpu.with_memory_space_constraint(grad, pltpu.VMEM), pltpu.with_memory_space_constraint(loss, pltpu.VMEM))
    return loss[0, 0], grad


def solution(mesh):
    names = ("yh", "core", "yl", "z", "x")
    split = Mesh(mesh.devices.reshape(4, 2, 2, 12, mesh.shape["tensor"]), names)
    in_specs = (P(IMAGES, None, None), P(), P(None, "x"), P("x", None), P(IMAGES, None))
    out_specs = (P(), P(IMAGES, None, "x"))
    return jax.shard_map(
        functools.partial(on_device, dict(split.shape)),
        mesh=split, in_specs=in_specs, out_specs=out_specs, check_vma=False,
    )
```

```python
import functools

import jax
import jax.numpy as jnp
from jax import lax
from jax.experimental import pallas as pl
from jax.experimental.pallas import tpu as pltpu
from jax.sharding import Mesh
from jax.sharding import PartitionSpec as P

IMAGES = ("yh", "core", "yl", "z")
MESH = pl.DeviceIdType.MESH

student_scale = 10.0
teacher_scale = 20.0
masked_value = -1000000000.0
F32, BF16 = jnp.float32, jnp.bfloat16
NT = (((1,), (1,)), ((), ()))
LANES = 128
BLOCK = 64


def as_tile(row):
    return jnp.concatenate([row[:, k * 128 : (k + 1) * 128] for k in range(8)], axis=0)


def normal_cdf(v):
    return 0.5 * (1.0 + lax.erf(v * 0.7071067811865476))


class Place:
    def __init__(self, sizes):
        self.x, self.z, self.c = (lax.axis_index(a) for a in ("x", "z", "core"))
        self.nx, self.nz = sizes["x"], sizes["z"]
        self.nl = sizes["yl"]
        self.ny = sizes["yh"] * sizes["yl"]
        self.y = lax.axis_index("yh") * self.nl + lax.axis_index("yl")
        self.row = (self.c * self.ny + self.y) * self.nz + self.z

    def at_x(self, d):
        return lax.rem(self.x + d, self.nx)

    def at_y(self, d):
        return lax.rem(self.y + d, self.ny)

    def at_z(self, d):
        return lax.rem(self.z + d, self.nz)

    def to_y(self, yy):
        return {"yh": yy // self.nl, "yl": lax.rem(yy, self.nl)}


def remote(src, dst, ss, rs, where):
    return pltpu.make_async_remote_copy(
        src_ref=src, dst_ref=dst, send_sem=ss, recv_sem=rs, device_id=where, device_id_type=MESH
    )


def step_kernel(sizes, pooled, gain_hbm, w1, w2, tea_hbm, out, loss_out,
                gain, tea, xv, nv, wv, w2v, wc, pv, sb, sl, xh, acc, meanv, rstdv,
                xbuf, cbuf, ub, tb, wide, U, T,
                local, done, xs, xr, cs, cr, ps, pr,
                uzs, uzr, uys, uyr, ucs, ucr, tzs, tzr, tys, tyr, tcs, tcr,
                wxs, wxr, prs, prr, wzs, wzr, wys, wyr, wds, wdr):
    me = Place(sizes)
    x, y, z, c = me.x, me.y, me.z, me.c
    nx, ny, nz = me.nx, me.ny, me.nz
    count = 2 * ny * nz
    tokens, width = xv.shape
    hid = wv.shape[1]
    emb = w2v.shape[1]
    cols = width // nx
    tiles = width // LANES

    get_tea = pltpu.make_async_copy(tea_hbm, tea, local.at[2 + nx])
    get_tea.start()
    get_gain = pltpu.make_async_copy(gain_hbm, gain, local.at[3 + nx])
    get_gain.start()

    get_x = []
    for k in range(tokens // BLOCK):
        t = pl.ds(k * BLOCK, BLOCK)
        get_x.append(pltpu.make_async_copy(pooled.at[0, t], xv.at[t], local.at[4 + nx + k]))
        get_x[-1].start()
    barrier = pltpu.get_barrier_semaphore()
    peers = (
        [{"x": me.at_x(d)} for d in range(1, nx)]
        + [{"z": me.at_z(d)} for d in range(1, nz)]
        + [me.to_y(me.at_y(d)) for d in range(1, ny)]
        + [{"core": 1 - c}]
    )
    for p in peers:
        pl.semaphore_signal(barrier, inc=1, device_id=p, device_id_type=MESH)

    get_w = []
    for k in range(nx):
        rows = pl.ds(k * cols, cols)
        get_w.append(pltpu.make_async_copy(w1.at[rows], wv.at[rows], local.at[1 + k]))
    get_w2 = pltpu.make_async_copy(w2, w2v, local.at[1 + nx])

    sent = []

    def send(src, dst, ss, rs, where):
        remote(src, dst, ss, rs, where).start()

    def arrive(ref, rs):
        remote(ref, ref, done.at[0], rs, {"core": 1 - c}).wait_recv()

    def left(ref, ss):
        sent.append(remote(ref, ref, ss, done.at[0], {"core": 1 - c}))

    get_gain.wait()
    for i in range(tokens // BLOCK):
        get_x[i].wait()
        if i == 1:
            for cp in get_w:
                cp.start()
            get_w2.start()
        r = slice(i * BLOCK, (i + 1) * BLOCK)
        total = jnp.zeros((BLOCK, LANES), F32)
        for k in range(tiles):
            total += xv[r, k * LANES : (k + 1) * LANES].astype(F32)
        m = jnp.broadcast_to(jnp.sum(total, axis=1, keepdims=True) / width, (BLOCK, LANES))
        squares = jnp.zeros((BLOCK, LANES), F32)
        for k in range(tiles):
            dev = xv[r, k * LANES : (k + 1) * LANES].astype(F32) - m
            squares += dev * dev
        var = jnp.sum(squares, axis=1, keepdims=True) / width
        rs = jnp.broadcast_to(lax.rsqrt(var + 1e-05), (BLOCK, LANES))
        meanv[r, :] = m
        rstdv[r, :] = rs
        for k in range(tiles):
            t = slice(k * LANES, (k + 1) * LANES)
            nv[r, t] = ((xv[r, t].astype(F32) - m) * rs * gain[:, t]).astype(BF16)

    def z_send(buf, ss, rs):
        for d in sorted(range(1, nz), key=lambda d: -min(d, nz - d)):
            send(buf.at[c, y, z], buf.at[c, y, z], ss, rs, {"z": me.at_z(d)})
        left(buf.at[c, y, pl.ds(0, nz - 1)], ss)

    def z_wait(buf, rs):
        arrive(buf.at[c, y, pl.ds(0, nz - 1)], rs)

    def y_send(buf, ss, rs):
        for d in (4, 3, 5, 2, 6, 1, 7):
            yy = me.at_y(d)
            send(buf.at[c, y], buf.at[c, y], ss, rs(y), me.to_y(yy))
        left(buf.at[c, pl.ds(0, ny - 1)], ss)

    quarter = cols // 4
    piece = quarter // 2
    half = piece // 2
    color = lax.rem(2 * y + z, 4)

    def place(k, part=0, length=piece):
        q = lax.rem(color + k, 4)
        return pl.ds(pl.multiple_of(q * quarter + c * piece + part, 16), length)


    first = 32

    def w_send(d, at, rows):
        xx = me.at_x(d)
        start = pl.multiple_of(xx * cols + color * quarter + c * piece + at, 16)
        send(w1.at[pl.ds(start, rows)], wc.at[x, place(0, at, rows)], wxs.at[0], wxr.at[x], {"x": xx})

    get_tea.wait()
    tvals = tea[...].astype(F32)
    tunit = tvals / jnp.sqrt(jnp.sum(tvals * tvals, axis=-1, keepdims=True) + 1e-06)
    tb[c, y, z] = as_tile(tunit).astype(BF16)
    g = gain[...]
    g_hi = g.astype(BF16)
    g_lo = (g - g_hi.astype(F32)).astype(BF16)
    sub16 = lax.broadcasted_iota(jnp.int32, (16, width), 0)
    nv[tokens:, :] = jnp.where(
        sub16 == 0, g_hi.astype(F32), jnp.where(sub16 == 1, g_lo.astype(F32), 0.0)
    ).astype(BF16)

    for k in range(nx):
        get_w[k].wait()
        if k == nx - 1:
            pl.semaphore_wait(barrier, len(peers))
            w_send(1, 0, first)
            w_send(3, 0, first)
            z_send(tb, tzs.at[0], tzr.at[0])
        t = slice(k * cols, (k + 1) * cols)
        part = jnp.dot(nv[:, t], wv[t, :], preferred_element_type=F32)
        if k == 0:
            pv[...] = part
        else:
            pv[...] += part

    pool = []
    for k in range(hid // LANES):
        t = slice(k * LANES, (k + 1) * LANES)

        def body(i, total, t=t):
            r = pl.ds(pl.multiple_of(i * BLOCK, BLOCK), BLOCK)
            p = pv[r, t]
            sb[x, r, t] = p.astype(BF16)
            act = p * normal_cdf(p)
            for j in range(BLOCK // 8):
                total += act[j * 8 : (j + 1) * 8]
            return total

        total = lax.fori_loop(0, tokens // BLOCK, body, jnp.zeros((8, LANES), F32))
        pool.append(jnp.sum(total, axis=0, keepdims=True))
    pool = jnp.concatenate(pool, axis=1) / tokens
    get_w2.wait()
    pool16 = jnp.broadcast_to(pool, (16, hid)).astype(BF16)
    xbuf[x, :, :emb] = jnp.dot(pool16, w2v[...], preferred_element_type=F32)[:1]
    xbuf[x, :, emb:] = pv[tokens : tokens + 1, :] + pv[tokens + 1 : tokens + 2, :]

    for d in (2, 1, 3):
        send(xbuf.at[x], xbuf.at[x], xs.at[0], xr.at[0], {"x": me.at_x(d)})
    left(xbuf.at[pl.ds(0, nx - 1)], xs.at[0])
    w_send(1, first, piece - first)
    w_send(3, first, piece - first)
    w_send(2, 0, piece)
    for d in (1, 3):
        send(sb.at[x], sb.at[x], ps.at[0], pr.at[d], {"x": me.at_x(d)})
    left(wc.at[0, pl.ds(0, 3 * piece)], wxs.at[0])
    left(sb.at[pl.ds(0, 2)], ps.at[0])
    arrive(xbuf.at[pl.ds(0, nx - 1)], xr.at[0])
    student = xbuf[0, :, :emb]
    for k in range(1, nx):
        student = student + xbuf[k, :, :emb]
    norm_s = jnp.sqrt(jnp.sum(student * student, axis=-1, keepdims=True) + 1e-06)
    unit32 = student / norm_s
    ub[c, y, z] = as_tile(unit32).astype(BF16)
    z_send(ub, uzs.at[0], uzr.at[0])
    z_wait(tb, tzr.at[0])
    y_send(tb, tys.at[0], lambda yy: tyr.at[0])

    def w_along_y(d):
        xx = me.at_x(d)
        low, high = wc.at[xx, place(0, 0, half)], wc.at[xx, place(0, half, half)]
        send(low, low, wys.at[0], wyr.at[d], me.to_y(me.at_y(1)))
        send(high, high, wys.at[0], wyr.at[d], me.to_y(me.at_y(ny - 1)))

    def w_from_x(d):
        xx = me.at_x(d)
        block = wc.at[xx, place(0)]
        arrive(block, wxr.at[xx])
        send(block, block, wzs.at[0], wzr.at[d], {"z": me.at_z(1)})
        send(block, block, wzs.at[0], wzr.at[d], {"z": me.at_z(nz - 1)})
        send(block, block, wds.at[0], wdr.at[d], {"core": 1 - c})

    w_from_x(1)
    w_along_y(1)
    w_from_x(3)

    def own_columns(k):
        return pl.ds(pl.multiple_of(x * cols + k * LANES, LANES), LANES)

    for k in range(cols // LANES):
        t = slice(k * LANES, (k + 1) * LANES)
        xh[:, t] = (xv[:, own_columns(k)].astype(F32) - meanv[...]) * rstdv[...]

    def slope_of(xx):
        for k in range(hid // LANES):
            t = slice(k * LANES, (k + 1) * LANES)

            @pl.loop(0, tokens // BLOCK)
            def _(i, t=t):
                r = pl.ds(pl.multiple_of(i * BLOCK, BLOCK), BLOCK)
                p = sb[xx, r, t].astype(F32)
                s = normal_cdf(p) + p * jnp.exp(-0.5 * p * p) * 0.3989422804014327
                sl[xx, r, t] = s.astype(BF16)

    slope_of(x)
    z_wait(ub, uzr.at[0])
    y_send(ub, uys.at[0], lambda yy: uyr.at[yy])
    w_from_x(2)

    def assemble(buf, dst):
        wide[...] = buf[...].astype(F32).reshape(count * 8, LANES)
        for s in range(8):
            dst[:, s * LANES : (s + 1) * LANES] = wide[pl.ds(s, count, stride=8), :].astype(BF16)

    down = lax.broadcasted_iota(jnp.int32, (count, count), 0)
    across = lax.broadcasted_iota(jnp.int32, (count, count), 1)
    diagonal = down == across
    lane = lax.broadcasted_iota(jnp.int32, (1, count), 1)

    def similarity(mat, scale):
        a = mat[...]
        s = lax.dot_general(a, a, NT, preferred_element_type=F32)
        s = jnp.where(diagonal, masked_value, scale * s)
        topr = jnp.max(s, axis=0, keepdims=True)
        lse_r = topr + jnp.log(jnp.sum(jnp.exp(s - topr), axis=0, keepdims=True))
        own = jnp.sum(jnp.where(down == me.row, s, 0.0), axis=0, keepdims=True)
        lse_own = jnp.sum(jnp.where(lane == me.row, lse_r, 0.0), axis=1, keepdims=True)
        return s, jnp.exp(own - lse_own), jnp.exp(own - lse_r)

    def log_probabilities(s):
        top = jnp.max(s, axis=1, keepdims=True)
        return s - (top + jnp.log(jnp.sum(jnp.exp(s - top), axis=1, keepdims=True)))

    arrive(tb.at[c, pl.ds(0, ny - 1)], tyr.at[0])
    send(tb.at[c], tb.at[c], tcs.at[0], tcr.at[0], {"core": 1 - c})
    left(tb.at[c], tcs.at[0])
    arrive(tb.at[1 - c], tcr.at[0])
    assemble(tb, T)
    t_log, p_row, p_col = similarity(T, teacher_scale)
    log_p = log_probabilities(t_log)
    prob_p = jnp.exp(log_p)

    for d in (0, 1, 7, 2, 6, 3, 5, 4):
        yy = me.at_y(d)
        if d:
            arrive(ub.at[c, yy], uyr.at[yy])
        send(ub.at[c, yy], ub.at[c, yy], ucs.at[0], ucr.at[0], {"core": 1 - c})
    left(ub.at[c], ucs.at[0])
    w_along_y(3)
    w_along_y(2)

    def w_across(d):
        xx = me.at_x(d)
        arrive(wc.at[xx, pl.ds(0, 2 * piece)], wzr.at[d])
        arrive(wc.at[xx, pl.ds(0, piece)], wyr.at[d])
        for k in (3, 1, 2):
            share = wc.at[xx, place(k)]
            send(share, share, wds.at[0], wdr.at[d], {"core": 1 - c})

    upper, lower = pl.ds(0, tokens // 2), pl.ds(tokens // 2, tokens // 2)
    after, before, far = me.at_x(1), me.at_x(3), me.at_x(2)
    arrive(sb.at[before], pr.at[1])
    arrive(sb.at[after], pr.at[3])
    send(sb.at[before, upper], sb.at[before, upper], prs.at[0], prr.at[0], {"x": after})
    send(sb.at[after, lower], sb.at[after, lower], prs.at[0], prr.at[1], {"x": before})
    w_across(1)
    arrive(ub.at[1 - c], ucr.at[0])
    assemble(ub, U)
    s_log, q_row, q_col = similarity(U, student_scale)
    sub = lax.broadcasted_iota(jnp.int32, (16, count), 0)
    d_row = (q_row - p_row) / count
    d_col = (q_col - p_col) / count
    both = jnp.where(sub == 0, d_row, jnp.where(sub == 1, d_col, 0.0)).astype(BF16)
    rows = jnp.dot(both, U[...], preferred_element_type=F32)
    d_unit = student_scale * jnp.sum(rows, axis=0, keepdims=True)
    along = jnp.sum(unit32 * d_unit, axis=-1, keepdims=True)
    d_student = (d_unit - unit32 * along) / norm_s
    d16 = jnp.broadcast_to(d_student, (16, emb)).astype(BF16)
    cbuf[x] = lax.dot_general(d16, w2v[...], NT, preferred_element_type=F32)[:1] / tokens
    for d in (2, 1, 3):
        send(cbuf.at[x], cbuf.at[x], cs.at[0], cr.at[x], {"x": me.at_x(d)})
    left(cbuf.at[pl.ds(0, nx - 1)], cs.at[0])

    sums = [jnp.zeros((tokens, LANES), F32), jnp.zeros((tokens, LANES), F32)]

    def scale_slope(xx):
        for k in range(hid // LANES):
            t = slice(k * LANES, (k + 1) * LANES)
            dp = (sl[xx, :, t].astype(F32) * cbuf[xx, :, t]).astype(BF16)
            sl[xx, :, t] = dp
            dp = dp.astype(F32)
            sums[0] += dp * xbuf[xx, :, emb + k * LANES : emb + (k + 1) * LANES]
            sums[1] += dp * sb[xx, :, t].astype(F32)

    w_across(3)
    scale_slope(x)
    step = 2 * LANES
    for j in range(cols // step):
        own = pl.ds(pl.multiple_of(x * cols + j * step, LANES), step)
        acc[:, j * step : (j + 1) * step] = lax.dot_general(
            sl[x], wv[own, :], NT, preferred_element_type=F32
        )
    w_across(2)
    slope_of(before)
    slope_of(after)
    arrive(sb.at[far, upper], prr.at[0])
    arrive(sb.at[far, lower], prr.at[1])
    slope_of(far)
    log_q = log_probabilities(s_log)
    terms = jnp.where(diagonal, 0.0, prob_p * (log_p - log_q))
    loss_out[...] = jnp.sum(jnp.sum(terms, axis=1, keepdims=True), axis=0, keepdims=True) / count
    for d in (1, 3, 2):
        xx = me.at_x(d)
        arrive(cbuf.at[xx], cr.at[xx])
        scale_slope(xx)
        arrive(wc.at[xx, pl.ds(0, 4 * piece)], wdr.at[d])
        if d != 2:
            for j in range(cols // step):
                span = slice(j * step, (j + 1) * step)
                acc[:, span] += lax.dot_general(sl[xx], wc[xx, span, :], NT, preferred_element_type=F32)
    mean_g = jnp.sum(sums[0], axis=1, keepdims=True) / width
    mean_c = jnp.sum(sums[1], axis=1, keepdims=True) / width

    for j in range(cols // step):
        span = slice(j * step, (j + 1) * step)
        grad = acc[:, span] + lax.dot_general(sl[far], wc[far, span, :], NT, preferred_element_type=F32)
        for h in range(2):
            k = 2 * j + h
            t = slice(k * LANES, (k + 1) * LANES)
            gt = grad[:, h * LANES : (h + 1) * LANES] * gain[:, own_columns(k)]
            out[0, :, t] = (rstdv[...] * (gt - mean_g - xh[:, t] * mean_c)).astype(BF16)
    left(sb.at[0], prs.at[0])
    left(wc.at[0, pl.ds(0, 6 * piece)], wzs.at[0])
    left(wc.at[0, pl.ds(0, 6 * half)], wys.at[0])
    left(wc.at[pl.ds(0, 3), pl.ds(0, 4 * piece)], wds.at[0])
    for cp in sent:
        cp.wait_send()


def store_kernel(grad, loss, grad_out, loss_out, sem):
    puts = [
        pltpu.make_async_copy(grad, grad_out, sem.at[0]),
        pltpu.make_async_copy(loss, loss_out, sem.at[1]),
    ]
    for put in puts:
        put.start()
    for put in puts:
        put.wait()


def on_device(sizes, pooled, layer_norm_gain, w_first, w_second, teacher):
    images, tokens, width = pooled.shape
    hid = w_first.shape[1]
    emb = w_second.shape[1]
    ny, nz, nx = sizes["yh"] * sizes["yl"], sizes["z"], sizes["x"]
    count = 2 * ny * nz
    cols = width // nx
    dma = lambda *n: pltpu.SemaphoreType.DMA(n)
    hbm, vmem = pl.BlockSpec(memory_space=pltpu.HBM), pl.BlockSpec(memory_space=pltpu.VMEM)
    grad, loss = pl.pallas_call(
        functools.partial(step_kernel, sizes),
        out_shape=(
            pltpu.VMEM((images, tokens, cols), BF16),
            pltpu.VMEM((1, 1), F32),
        ),
        in_specs=[hbm] * 5,
        out_specs=(vmem, vmem),
        scratch_shapes=[
            pltpu.VMEM((1, width), F32),
            pltpu.VMEM((1, emb), BF16),
            pltpu.VMEM((tokens, width), BF16),
            pltpu.VMEM((tokens + 16, width), BF16),
            pltpu.VMEM((width, hid), BF16),
            pltpu.VMEM((hid, emb), BF16),
            pltpu.VMEM((nx, cols, hid), BF16),
            pltpu.VMEM((tokens + 16, hid), F32),
            pltpu.VMEM((nx, tokens, hid), BF16),
            pltpu.VMEM((nx, tokens, hid), BF16),
            pltpu.VMEM((tokens, cols), F32),
            pltpu.VMEM((tokens, cols), F32),
            pltpu.VMEM((tokens, LANES), F32),
            pltpu.VMEM((tokens, LANES), F32),
            pltpu.VMEM((nx, 1, emb + hid), F32),
            pltpu.VMEM((nx, 1, hid), F32),
            pltpu.VMEM((2, ny, nz, 8, LANES), BF16),
            pltpu.VMEM((2, ny, nz, 8, LANES), BF16),
            pltpu.VMEM((count * 8, LANES), F32),
            pltpu.VMEM((count, emb), BF16),
            pltpu.VMEM((count, emb), BF16),
            dma(4 + 2 * nx), dma(1), dma(1), dma(1), dma(1), dma(nx), dma(1), dma(nx),
            dma(1), dma(1), dma(1), dma(ny), dma(1), dma(1),
            dma(1), dma(1), dma(1), dma(1), dma(1), dma(1),
            dma(1), dma(nx), dma(1), dma(2), dma(1), dma(nx), dma(1), dma(nx), dma(1), dma(nx),
        ],
        compiler_params=pltpu.CompilerParams(collective_id=0, has_side_effects=True, vmem_limit_bytes=48 * 2**20),
    )(*(pltpu.with_memory_space_constraint(a, pltpu.HBM) for a in (pooled, layer_norm_gain.reshape(1, width), w_first, w_second, teacher)))
    grad, loss = pl.pallas_call(
        store_kernel,
        out_shape=(jax.ShapeDtypeStruct((images, tokens, cols), BF16), jax.ShapeDtypeStruct((1, 1), F32)),
        in_specs=[vmem, vmem],
        out_specs=(hbm, hbm),
        scratch_shapes=[dma(2)],
        compiler_params=pltpu.CompilerParams(vmem_limit_bytes=2**20),
    )(pltpu.with_memory_space_constraint(grad, pltpu.VMEM), pltpu.with_memory_space_constraint(loss, pltpu.VMEM))
    return loss[0, 0], grad


def solution(mesh):
    names = ("yh", "core", "yl", "z", "x")
    split = Mesh(mesh.devices.reshape(4, 2, 2, 12, mesh.shape["tensor"]), names)
    in_specs = (P(IMAGES, None, None), P(), P(None, "x"), P("x", None), P(IMAGES, None))
    out_specs = (P(), P(IMAGES, None, "x"))
    return jax.shard_map(
        functools.partial(on_device, dict(split.shape)),
        mesh=split, in_specs=in_specs, out_specs=out_specs, check_vma=False,
    )
```

```python
import functools

import jax
import jax.numpy as jnp
from jax import lax
from jax.experimental import pallas as pl
from jax.experimental.pallas import tpu as pltpu
from jax.sharding import Mesh
from jax.sharding import PartitionSpec as P

IMAGES = ("yh", "core", "yl", "z")
MESH = pl.DeviceIdType.MESH

student_scale = 10.0
teacher_scale = 20.0
masked_value = -1000000000.0
F32, BF16 = jnp.float32, jnp.bfloat16
NT = (((1,), (1,)), ((), ()))
LANES = 128
BLOCK = 64


def as_tile(row):
    return jnp.concatenate([row[:, k * 128 : (k + 1) * 128] for k in range(8)], axis=0)


def normal_cdf(v):
    return 0.5 * (1.0 + lax.erf(v * 0.7071067811865476))


class Place:
    def __init__(self, sizes):
        self.x, self.z, self.c = (lax.axis_index(a) for a in ("x", "z", "core"))
        self.nx, self.nz = sizes["x"], sizes["z"]
        self.nl = sizes["yl"]
        self.ny = sizes["yh"] * sizes["yl"]
        self.y = lax.axis_index("yh") * self.nl + lax.axis_index("yl")
        self.row = (self.c * self.ny + self.y) * self.nz + self.z

    def at_x(self, d):
        return lax.rem(self.x + d, self.nx)

    def at_y(self, d):
        return lax.rem(self.y + d, self.ny)

    def at_z(self, d):
        return lax.rem(self.z + d, self.nz)

    def to_y(self, yy):
        return {"yh": yy // self.nl, "yl": lax.rem(yy, self.nl)}


def remote(src, dst, ss, rs, where):
    return pltpu.make_async_remote_copy(
        src_ref=src, dst_ref=dst, send_sem=ss, recv_sem=rs, device_id=where, device_id_type=MESH
    )


def step_kernel(sizes, pooled, gain_hbm, w1, w2, tea_hbm, out, loss_out,
                gain, tea, xv, nv, wv, w2v, wc, pv, sb, sl, xh, acc, meanv, rstdv,
                xbuf, cbuf, ub, tb, wide, U, T,
                local, done, xs, xr, cs, cr, ps, pr,
                uzs, uzr, uys, uyr, ucs, ucr, tzs, tzr, tys, tyr, tcs, tcr,
                wxs, wxr, prs, prr, wzs, wzr, wys, wyr, wds, wdr):
    me = Place(sizes)
    x, y, z, c = me.x, me.y, me.z, me.c
    nx, ny, nz = me.nx, me.ny, me.nz
    count = 2 * ny * nz
    tokens, width = xv.shape
    hid = wv.shape[1]
    emb = w2v.shape[1]
    cols = width // nx
    tiles = width // LANES

    get_tea = pltpu.make_async_copy(tea_hbm, tea, local.at[2 + nx])
    get_tea.start()
    get_gain = pltpu.make_async_copy(gain_hbm, gain, local.at[3 + nx])
    get_gain.start()

    get_x = []
    for k in range(tokens // BLOCK):
        t = pl.ds(k * BLOCK, BLOCK)
        get_x.append(pltpu.make_async_copy(pooled.at[0, t], xv.at[t], local.at[4 + nx + k]))
        get_x[-1].start()
    barrier = pltpu.get_barrier_semaphore()
    peers = (
        [{"x": me.at_x(d)} for d in range(1, nx)]
        + [{"z": me.at_z(d)} for d in range(1, nz)]
        + [me.to_y(me.at_y(d)) for d in range(1, ny)]
        + [{"core": 1 - c}]
    )
    for p in peers:
        pl.semaphore_signal(barrier, inc=1, device_id=p, device_id_type=MESH)

    get_w = []
    for k in range(nx):
        rows = pl.ds(k * cols, cols)
        get_w.append(pltpu.make_async_copy(w1.at[rows], wv.at[rows], local.at[1 + k]))
    get_w2 = pltpu.make_async_copy(w2, w2v, local.at[1 + nx])

    sent = []

    def send(src, dst, ss, rs, where):
        remote(src, dst, ss, rs, where).start()

    def arrive(ref, rs):
        remote(ref, ref, done.at[0], rs, {"core": 1 - c}).wait_recv()

    def left(ref, ss):
        sent.append(remote(ref, ref, ss, done.at[0], {"core": 1 - c}))

    get_gain.wait()
    get_tea.wait()
    tvals = tea[...].astype(F32)
    tunit = tvals / jnp.sqrt(jnp.sum(tvals * tvals, axis=-1, keepdims=True) + 1e-06)
    tb[c, y, z] = as_tile(tunit).astype(BF16)
    g = gain[...]
    g_hi = g.astype(BF16)
    g_lo = (g - g_hi.astype(F32)).astype(BF16)
    sub16 = lax.broadcasted_iota(jnp.int32, (16, width), 0)
    nv[tokens:, :] = jnp.where(
        sub16 == 0, g_hi.astype(F32), jnp.where(sub16 == 1, g_lo.astype(F32), 0.0)
    ).astype(BF16)

    for i in range(tokens // BLOCK):
        get_x[i].wait()
        if i == 1:
            for cp in get_w:
                cp.start()
            get_w2.start()
        r = slice(i * BLOCK, (i + 1) * BLOCK)
        total = jnp.zeros((BLOCK, LANES), F32)
        for k in range(tiles):
            total += xv[r, k * LANES : (k + 1) * LANES].astype(F32)
        m = jnp.broadcast_to(jnp.sum(total, axis=1, keepdims=True) / width, (BLOCK, LANES))
        squares = jnp.zeros((BLOCK, LANES), F32)
        for k in range(tiles):
            dev = xv[r, k * LANES : (k + 1) * LANES].astype(F32) - m
            squares += dev * dev
        var = jnp.sum(squares, axis=1, keepdims=True) / width
        rs = jnp.broadcast_to(lax.rsqrt(var + 1e-05), (BLOCK, LANES))
        meanv[r, :] = m
        rstdv[r, :] = rs
        for k in range(tiles):
            t = slice(k * LANES, (k + 1) * LANES)
            nv[r, t] = ((xv[r, t].astype(F32) - m) * rs * gain[:, t]).astype(BF16)

    def z_send(buf, ss, rs):
        for d in sorted(range(1, nz), key=lambda d: -min(d, nz - d)):
            send(buf.at[c, y, z], buf.at[c, y, z], ss, rs, {"z": me.at_z(d)})
        left(buf.at[c, y, pl.ds(0, nz - 1)], ss)

    def z_wait(buf, rs):
        arrive(buf.at[c, y, pl.ds(0, nz - 1)], rs)

    def y_send(buf, ss, rs):
        for d in (4, 3, 5, 2, 6, 1, 7):
            yy = me.at_y(d)
            send(buf.at[c, y], buf.at[c, y], ss, rs(y), me.to_y(yy))
        left(buf.at[c, pl.ds(0, ny - 1)], ss)

    quarter = cols // 4
    piece = quarter // 2
    half = piece // 2
    color = lax.rem(2 * y + z, 4)

    def place(k, part=0, length=piece):
        q = lax.rem(color + k, 4)
        return pl.ds(pl.multiple_of(q * quarter + c * piece + part, 16), length)


    first = 32

    def w_send(d, at, rows):
        xx = me.at_x(d)
        start = pl.multiple_of(xx * cols + color * quarter + c * piece + at, 16)
        send(w1.at[pl.ds(start, rows)], wc.at[x, place(0, at, rows)], wxs.at[0], wxr.at[x], {"x": xx})

    for k in range(nx):
        get_w[k].wait()
        if k == nx - 1:
            pl.semaphore_wait(barrier, len(peers))
            w_send(1, 0, first)
            w_send(3, 0, first)
            z_send(tb, tzs.at[0], tzr.at[0])
        t = slice(k * cols, (k + 1) * cols)
        part = jnp.dot(nv[:, t], wv[t, :], preferred_element_type=F32)
        if k == 0:
            pv[...] = part
        else:
            pv[...] += part

    pool = []
    for k in range(hid // LANES):
        t = slice(k * LANES, (k + 1) * LANES)

        def body(i, total, t=t):
            r = pl.ds(pl.multiple_of(i * BLOCK, BLOCK), BLOCK)
            p = pv[r, t]
            sb[x, r, t] = p.astype(BF16)
            act = p * normal_cdf(p)
            for j in range(BLOCK // 8):
                total += act[j * 8 : (j + 1) * 8]
            return total

        total = lax.fori_loop(0, tokens // BLOCK, body, jnp.zeros((8, LANES), F32))
        pool.append(jnp.sum(total, axis=0, keepdims=True))
    pool = jnp.concatenate(pool, axis=1) / tokens
    get_w2.wait()
    pool16 = jnp.broadcast_to(pool, (16, hid)).astype(BF16)
    xbuf[x, :, :emb] = jnp.dot(pool16, w2v[...], preferred_element_type=F32)[:1]
    xbuf[x, :, emb:] = pv[tokens : tokens + 1, :] + pv[tokens + 1 : tokens + 2, :]

    for d in (2, 1, 3):
        send(xbuf.at[x], xbuf.at[x], xs.at[0], xr.at[0], {"x": me.at_x(d)})
    left(xbuf.at[pl.ds(0, nx - 1)], xs.at[0])
    w_send(1, first, piece - first)
    w_send(3, first, piece - first)
    w_send(2, 0, piece)
    for d in (1, 3):
        send(sb.at[x], sb.at[x], ps.at[0], pr.at[d], {"x": me.at_x(d)})
    left(wc.at[0, pl.ds(0, 3 * piece)], wxs.at[0])
    left(sb.at[pl.ds(0, 2)], ps.at[0])
    arrive(xbuf.at[pl.ds(0, nx - 1)], xr.at[0])
    student = xbuf[0, :, :emb]
    for k in range(1, nx):
        student = student + xbuf[k, :, :emb]
    norm_s = jnp.sqrt(jnp.sum(student * student, axis=-1, keepdims=True) + 1e-06)
    unit32 = student / norm_s
    ub[c, y, z] = as_tile(unit32).astype(BF16)
    z_send(ub, uzs.at[0], uzr.at[0])
    z_wait(tb, tzr.at[0])
    y_send(tb, tys.at[0], lambda yy: tyr.at[0])

    def w_along_y(d):
        xx = me.at_x(d)
        low, high = wc.at[xx, place(0, 0, half)], wc.at[xx, place(0, half, half)]
        send(low, low, wys.at[0], wyr.at[d], me.to_y(me.at_y(1)))
        send(high, high, wys.at[0], wyr.at[d], me.to_y(me.at_y(ny - 1)))

    def w_from_x(d):
        xx = me.at_x(d)
        block = wc.at[xx, place(0)]
        arrive(block, wxr.at[xx])
        send(block, block, wzs.at[0], wzr.at[d], {"z": me.at_z(1)})
        send(block, block, wzs.at[0], wzr.at[d], {"z": me.at_z(nz - 1)})
        send(block, block, wds.at[0], wdr.at[d], {"core": 1 - c})

    w_from_x(1)
    w_along_y(1)
    w_from_x(3)

    def own_columns(k):
        return pl.ds(pl.multiple_of(x * cols + k * LANES, LANES), LANES)

    for k in range(cols // LANES):
        t = slice(k * LANES, (k + 1) * LANES)
        xh[:, t] = (xv[:, own_columns(k)].astype(F32) - meanv[...]) * rstdv[...]

    def slope_of(xx):
        for k in range(hid // LANES):
            t = slice(k * LANES, (k + 1) * LANES)

            @pl.loop(0, tokens // BLOCK)
            def _(i, t=t):
                r = pl.ds(pl.multiple_of(i * BLOCK, BLOCK), BLOCK)
                p = sb[xx, r, t].astype(F32)
                s = normal_cdf(p) + p * jnp.exp(-0.5 * p * p) * 0.3989422804014327
                sl[xx, r, t] = s.astype(BF16)

    slope_of(x)
    z_wait(ub, uzr.at[0])
    y_send(ub, uys.at[0], lambda yy: uyr.at[yy])
    w_from_x(2)

    def assemble(buf, dst, core):
        rows = count // 2
        r = pl.ds(pl.multiple_of(core * rows, 16), rows)
        wide[...] = buf[core].astype(F32).reshape(rows * 8, LANES)
        for s in range(8):
            dst[r, s * LANES : (s + 1) * LANES] = wide[pl.ds(s, rows, stride=8), :].astype(BF16)

    down = lax.broadcasted_iota(jnp.int32, (count, count), 0)
    across = lax.broadcasted_iota(jnp.int32, (count, count), 1)
    diagonal = down == across
    lane = lax.broadcasted_iota(jnp.int32, (1, count), 1)

    def similarity(mat, scale):
        a = mat[...]
        s = lax.dot_general(a, a, NT, preferred_element_type=F32)
        s = jnp.where(diagonal, masked_value, scale * s)
        topr = jnp.max(s, axis=0, keepdims=True)
        lse_r = topr + jnp.log(jnp.sum(jnp.exp(s - topr), axis=0, keepdims=True))
        own = jnp.sum(jnp.where(down == me.row, s, 0.0), axis=0, keepdims=True)
        lse_own = jnp.sum(jnp.where(lane == me.row, lse_r, 0.0), axis=1, keepdims=True)
        return s, jnp.exp(own - lse_own), jnp.exp(own - lse_r)

    def log_probabilities(s):
        top = jnp.max(s, axis=1, keepdims=True)
        return s - (top + jnp.log(jnp.sum(jnp.exp(s - top), axis=1, keepdims=True)))

    arrive(tb.at[c, pl.ds(0, ny - 1)], tyr.at[0])
    send(tb.at[c], tb.at[c], tcs.at[0], tcr.at[0], {"core": 1 - c})
    left(tb.at[c], tcs.at[0])
    assemble(tb, T, c)
    arrive(tb.at[1 - c], tcr.at[0])
    assemble(tb, T, 1 - c)
    t_log, p_row, p_col = similarity(T, teacher_scale)
    log_p = log_probabilities(t_log)
    prob_p = jnp.exp(log_p)

    for d in (0, 1, 7, 2, 6, 3, 5, 4):
        yy = me.at_y(d)
        if d:
            arrive(ub.at[c, yy], uyr.at[yy])
        send(ub.at[c, yy], ub.at[c, yy], ucs.at[0], ucr.at[0], {"core": 1 - c})
    left(ub.at[c], ucs.at[0])
    w_along_y(3)
    w_along_y(2)

    def w_across(d):
        xx = me.at_x(d)
        arrive(wc.at[xx, pl.ds(0, 2 * piece)], wzr.at[d])
        arrive(wc.at[xx, pl.ds(0, piece)], wyr.at[d])
        for k in (3, 1, 2):
            share = wc.at[xx, place(k)]
            send(share, share, wds.at[0], wdr.at[d], {"core": 1 - c})

    upper, lower = pl.ds(0, tokens // 2), pl.ds(tokens // 2, tokens // 2)
    after, before, far = me.at_x(1), me.at_x(3), me.at_x(2)
    arrive(sb.at[before], pr.at[1])
    arrive(sb.at[after], pr.at[3])
    send(sb.at[before, upper], sb.at[before, upper], prs.at[0], prr.at[0], {"x": after})
    send(sb.at[after, lower], sb.at[after, lower], prs.at[0], prr.at[1], {"x": before})
    w_across(1)
    assemble(ub, U, c)
    arrive(ub.at[1 - c], ucr.at[0])
    assemble(ub, U, 1 - c)
    s_log, q_row, q_col = similarity(U, student_scale)
    sub = lax.broadcasted_iota(jnp.int32, (16, count), 0)
    d_row = (q_row - p_row) / count
    d_col = (q_col - p_col) / count
    both = jnp.where(sub == 0, d_row, jnp.where(sub == 1, d_col, 0.0)).astype(BF16)
    rows = jnp.dot(both, U[...], preferred_element_type=F32)
    d_unit = student_scale * jnp.sum(rows, axis=0, keepdims=True)
    along = jnp.sum(unit32 * d_unit, axis=-1, keepdims=True)
    d_student = (d_unit - unit32 * along) / norm_s
    d16 = jnp.broadcast_to(d_student, (16, emb)).astype(BF16)
    cbuf[x] = lax.dot_general(d16, w2v[...], NT, preferred_element_type=F32)[:1] / tokens
    for d in (2, 1, 3):
        send(cbuf.at[x], cbuf.at[x], cs.at[0], cr.at[x], {"x": me.at_x(d)})
    left(cbuf.at[pl.ds(0, nx - 1)], cs.at[0])

    sums = [jnp.zeros((tokens, LANES), F32), jnp.zeros((tokens, LANES), F32)]

    def scale_slope(xx):
        for k in range(hid // LANES):
            t = slice(k * LANES, (k + 1) * LANES)
            dp = (sl[xx, :, t].astype(F32) * cbuf[xx, :, t]).astype(BF16)
            sl[xx, :, t] = dp
            dp = dp.astype(F32)
            sums[0] += dp * xbuf[xx, :, emb + k * LANES : emb + (k + 1) * LANES]
            sums[1] += dp * sb[xx, :, t].astype(F32)

    w_across(3)
    scale_slope(x)
    step = 2 * LANES
    for j in range(cols // step):
        own = pl.ds(pl.multiple_of(x * cols + j * step, LANES), step)
        acc[:, j * step : (j + 1) * step] = lax.dot_general(
            sl[x], wv[own, :], NT, preferred_element_type=F32
        )
    w_across(2)
    slope_of(before)
    slope_of(after)
    arrive(sb.at[far, upper], prr.at[0])
    arrive(sb.at[far, lower], prr.at[1])
    slope_of(far)
    log_q = log_probabilities(s_log)
    terms = jnp.where(diagonal, 0.0, prob_p * (log_p - log_q))
    loss_out[...] = jnp.sum(jnp.sum(terms, axis=1, keepdims=True), axis=0, keepdims=True) / count
    for d in (1, 3, 2):
        xx = me.at_x(d)
        arrive(cbuf.at[xx], cr.at[xx])
        scale_slope(xx)
        arrive(wc.at[xx, pl.ds(0, 4 * piece)], wdr.at[d])
        if d != 2:
            for j in range(cols // step):
                span = slice(j * step, (j + 1) * step)
                acc[:, span] += lax.dot_general(sl[xx], wc[xx, span, :], NT, preferred_element_type=F32)
    mean_g = jnp.sum(sums[0], axis=1, keepdims=True) / width
    mean_c = jnp.sum(sums[1], axis=1, keepdims=True) / width

    for j in range(cols // step):
        span = slice(j * step, (j + 1) * step)
        grad = acc[:, span] + lax.dot_general(sl[far], wc[far, span, :], NT, preferred_element_type=F32)
        for h in range(2):
            k = 2 * j + h
            t = slice(k * LANES, (k + 1) * LANES)
            gt = grad[:, h * LANES : (h + 1) * LANES] * gain[:, own_columns(k)]
            out[0, :, t] = (rstdv[...] * (gt - mean_g - xh[:, t] * mean_c)).astype(BF16)
    left(sb.at[0], prs.at[0])
    left(wc.at[0, pl.ds(0, 6 * piece)], wzs.at[0])
    left(wc.at[0, pl.ds(0, 6 * half)], wys.at[0])
    left(wc.at[pl.ds(0, 3), pl.ds(0, 4 * piece)], wds.at[0])
    for cp in sent:
        cp.wait_send()


def store_kernel(grad, loss, grad_out, loss_out, sem):
    puts = [pltpu.make_async_copy(loss, loss_out, sem.at[0])]
    for k in range(grad.shape[1] // BLOCK):
        rows = (slice(None), pl.ds(k * BLOCK, BLOCK))
        puts.append(pltpu.make_async_copy(grad.at[rows], grad_out.at[rows], sem.at[1 + k]))
    for put in puts:
        put.start()
    for put in puts:
        put.wait()


def on_device(sizes, pooled, layer_norm_gain, w_first, w_second, teacher):
    images, tokens, width = pooled.shape
    hid = w_first.shape[1]
    emb = w_second.shape[1]
    ny, nz, nx = sizes["yh"] * sizes["yl"], sizes["z"], sizes["x"]
    count = 2 * ny * nz
    cols = width // nx
    dma = lambda *n: pltpu.SemaphoreType.DMA(n)
    hbm, vmem = pl.BlockSpec(memory_space=pltpu.HBM), pl.BlockSpec(memory_space=pltpu.VMEM)
    grad, loss = pl.pallas_call(
        functools.partial(step_kernel, sizes),
        out_shape=(
            pltpu.VMEM((images, tokens, cols), BF16),
            pltpu.VMEM((1, 1), F32),
        ),
        in_specs=[hbm] * 5,
        out_specs=(vmem, vmem),
        scratch_shapes=[
            pltpu.VMEM((1, width), F32),
            pltpu.VMEM((1, emb), BF16),
            pltpu.VMEM((tokens, width), BF16),
            pltpu.VMEM((tokens + 16, width), BF16),
            pltpu.VMEM((width, hid), BF16),
            pltpu.VMEM((hid, emb), BF16),
            pltpu.VMEM((nx, cols, hid), BF16),
            pltpu.VMEM((tokens + 16, hid), F32),
            pltpu.VMEM((nx, tokens, hid), BF16),
            pltpu.VMEM((nx, tokens, hid), BF16),
            pltpu.VMEM((tokens, cols), F32),
            pltpu.VMEM((tokens, cols), F32),
            pltpu.VMEM((tokens, LANES), F32),
            pltpu.VMEM((tokens, LANES), F32),
            pltpu.VMEM((nx, 1, emb + hid), F32),
            pltpu.VMEM((nx, 1, hid), F32),
            pltpu.VMEM((2, ny, nz, 8, LANES), BF16),
            pltpu.VMEM((2, ny, nz, 8, LANES), BF16),
            pltpu.VMEM((count * 4, LANES), F32),
            pltpu.VMEM((count, emb), BF16),
            pltpu.VMEM((count, emb), BF16),
            dma(4 + 2 * nx), dma(1), dma(1), dma(1), dma(1), dma(nx), dma(1), dma(nx),
            dma(1), dma(1), dma(1), dma(ny), dma(1), dma(1),
            dma(1), dma(1), dma(1), dma(1), dma(1), dma(1),
            dma(1), dma(nx), dma(1), dma(2), dma(1), dma(nx), dma(1), dma(nx), dma(1), dma(nx),
        ],
        compiler_params=pltpu.CompilerParams(collective_id=0, has_side_effects=True, vmem_limit_bytes=48 * 2**20),
    )(*(pltpu.with_memory_space_constraint(a, pltpu.HBM) for a in (pooled, layer_norm_gain.reshape(1, width), w_first, w_second, teacher)))
    grad, loss = pl.pallas_call(
        store_kernel,
        out_shape=(jax.ShapeDtypeStruct((images, tokens, cols), BF16), jax.ShapeDtypeStruct((1, 1), F32)),
        in_specs=[vmem, vmem],
        out_specs=(hbm, hbm),
        scratch_shapes=[dma(1 + tokens // BLOCK)],
        compiler_params=pltpu.CompilerParams(vmem_limit_bytes=2**20),
    )(pltpu.with_memory_space_constraint(grad, pltpu.VMEM), pltpu.with_memory_space_constraint(loss, pltpu.VMEM))
    return loss[0, 0], grad


def solution(mesh):
    names = ("yh", "core", "yl", "z", "x")
    split = Mesh(mesh.devices.reshape(4, 2, 2, 12, mesh.shape["tensor"]), names)
    in_specs = (P(IMAGES, None, None), P(), P(None, "x"), P("x", None), P(IMAGES, None))
    out_specs = (P(), P(IMAGES, None, "x"))
    return jax.shard_map(
        functools.partial(on_device, dict(split.shape)),
        mesh=split, in_specs=in_specs, out_specs=out_specs, check_vma=False,
    )
```
